32 devices in a mesh: row: 4 (over y, core), col: 8 (over z, x).
Axes of the slice: x: 2, y: 2, z: 4, core: 2. Of those that a mesh axis runs over, the one named last changes fastest.
Arguments:
- kernel: float32 [4, 4, 256, 2, 8, 256], P(None, 'row', None, None, 'col'), may hold values from -40 to 40, as said below
Outputs:
- trailing: float32 [4, 4, 256, 2, 8, 256], P(None, 'row', None, None, 'col')
- panels: float32 [4, 4, 256, 3, 256], P(None, 'row')
The draws below stay inside these ranges and needn't reach their ends.
Inputs may be any that keep to these rules, and one draw needn't show every extreme that they name: kernel is symmetric and positive definite with smallest eigenvalue at least 1.
All inputs are finite; a program needn't handle non-finite values.
Results may differ from the reference program's by a relative error of at most 0.0003.
Values sent between devices are 32-bit elements; how exact they have to be, the bound alone decides.
A program may use at most 128 MiB of HBM per device.

```python
import jax
import jax.numpy as jnp
from jax import lax

TILE = 256
FEATURES = 1024
STEPS = 3
COL_TILES = 2
TILES = 16
ROW_TILES = 4
ORDER = 4096


def draw_kernel(key, part):
    key_main = jax.random.fold_in(key, 11)
    features = jax.random.normal(key_main, (ORDER, FEATURES), jnp.float32)
    gram = jnp.dot(features, features.T, precision=lax.Precision.HIGHEST) / FEATURES
    gram = gram + jnp.eye(ORDER, dtype=jnp.float32)
    return gram.reshape(ROW_TILES, TILES // ROW_TILES, TILE, COL_TILES, TILES // COL_TILES, TILE)


def setup_inputs(seed: int = 0) -> dict:
    streams_of = jax.random.split(jax.random.key(seed), 2)
    kernel = draw_kernel(jax.random.fold_in(streams_of[1], 71), 0)
    return dict(kernel=kernel)


def reference(kernel):
    shape_in = kernel.shape
    order = shape_in[0] * shape_in[1] * shape_in[2]
    tile_size = shape_in[2]
    working = kernel.reshape(order, order)
    identity = jnp.eye(tile_size, dtype=jnp.float32)
    row_ids = jnp.arange(order)
    collected = []
    for panel_step in range(STEPS):
        start = panel_step * tile_size
        finish = start + tile_size
        factor = jnp.linalg.cholesky(working[start:finish, start:finish])
        inverse = lax.linalg.triangular_solve(factor, identity, left_side=True, lower=True)
        panel = jnp.dot(working[:, start:finish], inverse.T, precision=lax.Precision.HIGHEST)
        panel = jnp.where((row_ids >= start)[:, None], panel, jnp.float32(0.0))
        collected.append(panel)
        lower = panel[finish:]
        updated = working[finish:, finish:] - jnp.dot(lower, lower.T, precision=lax.Precision.HIGHEST)
        working = jnp.zeros((order, order), jnp.float32).at[finish:, finish:].set(updated)
    trailing = working.reshape(shape_in)
    panels = jnp.stack(collected, axis=1).reshape(shape_in[0], shape_in[1], tile_size, STEPS, tile_size)
    return (trailing, panels)
```

```python
import functools

import jax
import jax.numpy as jnp
from jax import lax
from jax.experimental import pallas as pl
from jax.experimental.pallas import tpu as pltpu
from jax.sharding import PartitionSpec as P

STEPS = 3
PANEL = 16
LANES = 128
SKEW = 2
LAG = 3
RS_AT = 5
PACE = (1, 2)
CS_AT = 10
CS_LAG = 3
PIECES = 2
MESH = pl.DeviceIdType.MESH
F32 = jnp.float32
BF16 = jnp.bfloat16
LOWER = [(i, j) for j in range(STEPS) for i in range(j, STEPS)]
SLOT = {ij: n for n, ij in enumerate(LOWER)}


def split_col(cols):
    width = 1
    while width * width * 4 <= cols:
        width *= 2
    return width, cols // width


def dot_nt(p, q):
    return lax.dot_general(p, q, (((1,), (1,)), ((), ())), precision=lax.Precision.HIGHEST, preferred_element_type=F32)


def dot_nn(p, q):
    return lax.dot_general(p, q, (((1,), (0,)), ((), ())), precision=lax.Precision.HIGHEST, preferred_element_type=F32)


def invert_factor(w_ref, between):
    T = w_ref.shape[0]
    b = PANEL
    lane = lax.broadcasted_iota(jnp.int32, (b, T), 1)
    sub = lax.broadcasted_iota(jnp.int32, (b, T), 0)
    row = lax.broadcasted_iota(jnp.int32, (T, T), 0)
    col = lax.broadcasted_iota(jnp.int32, (T, T), 1)

    def body(p, carry):
        base = pl.multiple_of(p * b, b)
        R = w_ref[pl.ds(base, b), :]
        E = jnp.where(lane == base + sub, F32(1.0), F32(0.0))
        cols = []
        for j in range(b):
            picked = jnp.sum(jnp.where(lane == base + j, R, F32(0.0)), axis=1, keepdims=True)
            cols.append(jnp.broadcast_to(picked, (b, T)))
        diag = jnp.ones((b, T), F32)
        for j in range(b):
            d = jnp.broadcast_to(cols[j][j : j + 1, :], (b, T))
            diag = jnp.where(sub == j, d, diag)
            if j == b - 1:
                break
            w = jnp.where(sub > j, cols[j] * (F32(1.0) / d), F32(0.0))
            for i in range(j + 1, b):
                cols[i] = cols[i] - w * cols[i][j : j + 1, :]
            R = R - w * R[j : j + 1, :]
            E = E - w * E[j : j + 1, :]
        scale = lax.rsqrt(diag)
        R = R * scale
        E = E * scale
        V = jnp.where((lane >= base) & (lane < base + b), E, R)
        coef = jnp.where(lane >= base + b, R, F32(0.0))
        update = lax.dot_general(
            coef, V, (((0,), (0,)), ((), ())), precision=lax.Precision.HIGHEST, preferred_element_type=F32
        )
        drop = (row >= base + b) & (col >= base) & (col < base + b)
        w_ref[...] = jnp.where(drop, F32(0.0), w_ref[...]) - update
        w_ref[pl.ds(base, b), :] = V
        return carry

    def block(p, carry):
        between(p)
        return body(p, carry)

    lax.fori_loop(0, T // b, block, 0)
    w_ref[...] = jnp.where(row >= col, w_ref[...], F32(0.0))


def table(n, values):
    total = 0
    for m, value in enumerate(values):
        if value:
            total = total + jnp.where(n == m, value, 0)
    return total


def read_tile(x_ref, a, b, B, T):
    halves_ = T // LANES
    stride = B * halves_
    start = a * (T * stride) + b * halves_
    return [x_ref[pl.ds(start + h, T, stride=stride), :] for h in range(halves_)]


def load_tile(x_ref, a, b, B, T):
    return jnp.concatenate(read_tile(x_ref, a, b, B, T), axis=1)


def move_tile(dst, x_ref, a, b, B, T):
    for h, value in enumerate(read_tile(x_ref, a, b, B, T)):
        dst[:, h * LANES : (h + 1) * LANES] = value


def lead_kernel(
    R, C, A, B, T, x_ref, m_ref, rs_ref, cs_ref, own_ref, ld_ref, w_ref,
    scat_send, ld_send, ld_sem, ldy_sem, ldc_sem, rs_sem, rs_send, cs_sem, cs_send,
):
    X, Z = split_col(C)
    K = 2 if R % 2 == 0 else 1
    Y = R // K
    r, c = lax.axis_index("row"), lax.axis_index("col")
    z, x = lax.div(c, X), lax.rem(c, X)
    y, core = lax.div(r, K), lax.rem(r, K)
    chunk = T // R
    items = A * STEPS * PIECES
    tiles = len(LOWER)
    blocks = T // PANEL

    def remote(src, send_sem, recv_sem, dev):
        return pltpu.make_async_remote_copy(
            src_ref=src, dst_ref=src, send_sem=send_sem, recv_sem=recv_sem, device_id=dev, device_id_type=MESH
        )

    def arrived(dst, recv_sem):
        remote(dst, scat_send.at[0, 0], recv_sem, (lax.rem(r + 1, R), c)).wait_recv()

    def across(step):
        return lax.rem(y + step, Y) * K + core, c

    def beside(step):
        return y * K + lax.rem(core + step, K), c

    def part(ref, q):
        return ref.at[pl.ds(pl.multiple_of(q * chunk, chunk), chunk), :]

    def owner(n):
        i, j = table(n, [i for i, _ in LOWER]), table(n, [j for _, j in LOWER])
        return lax.rem(i, R), lax.rem(j, C)

    def scatter(n):
        ri, cj = owner(n)
        for step in range(1, R):
            q = lax.rem(r + step, R)
            yield pltpu.make_async_remote_copy(
                src_ref=part(own_ref.at[n], q), dst_ref=part(ld_ref.at[n], q),
                send_sem=scat_send.at[n, step - 1], recv_sem=ld_sem.at[n], device_id=(q, c), device_id_type=MESH,
            )

    for n, (i, j) in enumerate(LOWER):

        @pl.when((r == i % R) & (c == j % C))
        def _():
            move_tile(own_ref.at[n], x_ref, i // R, j // C, B, T)
            part(ld_ref.at[n], r)[...] = part(own_ref.at[n], r)[...]
            for copy in scatter(n):
                copy.start()

    def lead_out(n):
        _, source = owner(n)
        zs, xs = lax.div(source, X), lax.rem(source, X)
        lane = lax.rem(n + r, X)
        on = x == lane
        slot = part(ld_ref.at[n], r)

        def line(m, dev):
            return remote(slot, ld_send.at[n, m], ld_sem.at[n], dev)

        yield on & (z >= zs) & (z + 1 < Z), line(0, (r, lax.rem(c + X, C)))
        yield on & (z <= zs) & (z > 0), line(1, (r, lax.rem(c + C - X, C)))
        yield (c == source) & (xs != lane), line(2, (r, zs * X + lane))
        for step in range(1, X):
            other = lax.rem(lane + step, X)
            yield on & jnp.logical_not((z == zs) & (other == xs)), line(2 + step, (r, z * X + other))
        for step in range(1, Y):
            yield r >= 0, remote(slot, ld_send.at[n, X + 1 + step], ldy_sem.at[n, step - 1], across(step))
        for step in range(1, K):
            yield r >= 0, remote(slot, ld_send.at[n, X + Y + step], ldc_sem.at[n, step - 1, 0], beside(step))

    def lead_on(n):
        for step in range(1, Y):
            slot = part(ld_ref.at[n], lax.rem(y + Y - step, Y) * K + core)
            for side in range(1, K):
                m = X + Y + K + (step - 1) * (K - 1) + side - 1
                yield step, slot, remote(slot, ld_send.at[n, m], ldc_sem.at[n, side - 1, step], beside(side))
            if K == 1:
                yield step, slot, None

    def lead_first(n):
        ri, cj = owner(n)

        @pl.when((r != ri) | (c != cj))
        def _():
            arrived(part(ld_ref.at[n], r), ld_sem.at[n])

        for go, copy in lead_out(n):
            pl.when(go)(copy.start)

    def lead_second(n):
        for step, slot, copy in lead_on(n):
            arrived(slot, ldy_sem.at[n, step - 1])
            if copy is not None:
                copy.start()

    def lead_third(n):
        for side in range(1, K):
            for step in range(Y):
                q = lax.rem(y + Y - step, Y) * K + lax.rem(core + K - side, K)
                arrived(part(ld_ref.at[n], q), ldc_sem.at[n, side - 1, step])
        w_ref[n] = ld_ref[n]

    def lead_end(n, carry):
        ri, cj = owner(n)
        for copy in scatter(n):
            pl.when((r == ri) & (c == cj))(copy.wait_send)
        for go, copy in lead_out(n):
            pl.when(go)(copy.wait_send)
        for _, _, copy in lead_on(n):
            if copy is not None:
                copy.wait_send()
        return carry

    def item(m):
        tile, piece = lax.div(m, PIECES), lax.rem(m, PIECES)
        k, a = lax.rem(tile, STEPS), A - 1 - lax.div(tile, STEPS)
        source = lax.rem(k, C)
        zs, xs = lax.div(source, X), lax.rem(source, X)
        lane = lax.rem(k + a, X)
        return k, a, piece, source, zs, xs, lane

    def need(m):
        return item(m)[1] * R + r >= STEPS

    def piece_of(m):
        k, a, piece = item(m)[:3]
        rows = T // PIECES
        return rs_ref.at[k, a, pl.ds(pl.multiple_of(piece * rows, rows), rows), :]

    def spread(m):
        _, _, _, source, zs, xs, lane = item(m)
        on = (x == lane) & need(m)
        slot = piece_of(m)

        def copy(n, dev):
            return remote(slot, rs_send.at[m, n], rs_sem.at[m], dev)

        yield (c == source) & (xs != lane) & need(m), copy(0, (r, lax.rem(zs * X + lane, C)))
        yield on & (z >= zs) & (z + 1 < Z), copy(1, (r, lax.rem(c + X, C)))
        yield on & (z <= zs) & (z > 0), copy(2, (r, lax.rem(c + C - X, C)))
        for step in range(1, X):
            other = lax.rem(lane + step, X)
            yield on & jnp.logical_not((z == zs) & (other == xs)), copy(2 + step, (r, z * X + other))

    def forward(m):
        _, _, _, source, _, _, lane = item(m)

        @pl.when(((x == lane) | (c == source)) & need(m))
        def _():
            pl.when(c != source)(lambda: arrived(piece_of(m), rs_sem.at[m]))
            for go, out in spread(m):
                pl.when(go)(out.start)

    def col_at(e):
        k, b = lax.div(e, B), lax.rem(e, B)
        source = lax.rem(k, R)
        return cs_ref.at[k, b], source, lax.div(source, K), lax.rem(source, K)

    def col_out(e):
        slot, source, _, _ = col_at(e)
        for step in range(1, Y):
            yield r == source, remote(slot, cs_send.at[e, step - 1], cs_sem.at[e], across(step))

    def col_on(e):
        slot, _, _, kc = col_at(e)
        for step in range(1, K):
            yield core == kc, remote(slot, cs_send.at[e, Y + step - 2], cs_sem.at[e], beside(step))

    def col_first(e):
        for go, copy in col_out(e):
            pl.when(go)(copy.start)

    def col_second(e):
        slot, source, _, kc = col_at(e)

        @pl.when(core == kc)
        def _():
            pl.when(r != source)(lambda: arrived(slot, cs_sem.at[e]))
            for _, copy in col_on(e):
                copy.start()

    def col_end(e, carry):
        slot, _, _, kc = col_at(e)
        pl.when(core != kc)(lambda: arrived(slot, cs_sem.at[e]))
        for copies in (col_out(e), col_on(e)):
            for go, copy in copies:
                pl.when(go)(copy.wait_send)
        return carry

    cols = STEPS * B
    skew = SKEW * z

    def paced(v):
        return jnp.clip(lax.div(jnp.maximum(v, 0) * PACE[0], PACE[1]), 0, items)

    def slot_work(u):
        v = u - skew

        @pl.when((v >= 0) & (v < tiles - 1))
        def _():
            lead_first(v + 1)

        @pl.when((v >= LAG) & (v < tiles - 1 + LAG))
        def _():
            lead_second(v + 1 - LAG)

        lax.fori_loop(paced(v - RS_AT), paced(v - RS_AT + 1), lambda m, s: (forward(m), s)[1], 0)
        e, f = v - CS_AT, v - CS_AT - CS_LAG
        pl.when((e >= 0) & (e < cols))(lambda: col_first(e))
        pl.when((f >= 0) & (f < cols))(lambda: col_second(f))

    lead_first(0)
    for k in range(STEPS):

        def own_rows(a, carry, k=k):
            pl.when(a * R + r >= STEPS)(lambda: move_tile(rs_ref.at[k, a], x_ref, a, k // C, B, T))
            return carry

        @pl.when(c == k % C)
        def _():
            lax.fori_loop(0, A, own_rows, 0)

        for b in range(B):
            pl.when(r == k % R)(lambda: move_tile(cs_ref.at[k, b], x_ref, k // R, b, B, T))
    lead_second(0)
    lead_third(0)
    for k in range(STEPS):
        invert_factor(w_ref.at[SLOT[k, k]], lambda p, k=k: slot_work(k * blocks + p))
        inv = w_ref[SLOT[k, k]]
        if k == 0:
            for n in range(1, tiles):
                lead_third(n)
            for i in range(STEPS):

                @pl.when(r == i % R)
                def _():
                    for j in range(STEPS):
                        rs_ref[j, i // R] = ld_ref[SLOT[i, j]] if j <= i else jnp.zeros((T, T), F32)

        for i in range(k + 1, STEPS):
            w_ref[SLOT[i, k]] = dot_nt(w_ref[SLOT[i, k]], inv)
        for j in range(k + 1, STEPS):
            for i in range(j, STEPS):
                w_ref[SLOT[i, j]] = w_ref[SLOT[i, j]] - dot_nt(w_ref[SLOT[i, k]], w_ref[SLOT[j, k]])
    for k in range(STEPS):
        m_ref[SLOT[k, k]] = w_ref[SLOT[k, k]]
        for i in range(k + 1, STEPS):
            total = dot_nn(w_ref[SLOT[i, k]], m_ref[SLOT[k, k]])
            for j in range(k + 1, i):
                total = total + dot_nn(w_ref[SLOT[i, j]], m_ref[SLOT[j, k]])
            m_ref[SLOT[i, k]] = -dot_nn(w_ref[SLOT[i, i]], total)

    last = SKEW * (Z - 1) + RS_AT + -(-items * PACE[1] // PACE[0])
    last = max(last, SKEW * (Z - 1) + CS_AT + CS_LAG + cols)
    lax.fori_loop(STEPS * blocks, max(last, STEPS * blocks), lambda u, s: (slot_work(u), s)[1], 0)

    def finish_item(m, carry):
        _, _, _, source, _, _, lane = item(m)
        pl.when((x != lane) & (c != source) & need(m))(lambda: arrived(piece_of(m), rs_sem.at[m]))
        for go, out in spread(m):
            pl.when(go)(out.wait_send)
        return carry

    lax.fori_loop(0, items, finish_item, 0)
    lax.fori_loop(0, cols, col_end, 0)
    lax.fori_loop(0, tiles, lead_end, 0)


def lead(tiles, R, C, A, B, T):
    X, _ = split_col(C)
    K = 2 if R % 2 == 0 else 1
    Y = R // K
    n = len(LOWER)
    items = STEPS * A * PIECES
    vmem = pl.BlockSpec(memory_space=pltpu.VMEM)
    dma = pltpu.SemaphoreType.DMA
    return pl.pallas_call(
        functools.partial(lead_kernel, R, C, A, B, T),
        name="lead",
        out_shape=(
            jax.ShapeDtypeStruct((n, T, T), F32),
            jax.ShapeDtypeStruct((STEPS, A, T, T), F32),
            jax.ShapeDtypeStruct((STEPS, B, T, T), F32),
        ),
        in_specs=[vmem],
        out_specs=(vmem, vmem, vmem),
        scratch_shapes=[
            pltpu.VMEM((n, T, T), F32),
            pltpu.VMEM((n, T, T), F32),
            pltpu.VMEM((n, T, T), F32),
            dma((n, max(R - 1, 1))), dma((n, X + Y + K + Y * K)), dma((n,)), dma((n, Y)), dma((n, K, Y)),
            dma((items,)), dma((items, X + 2)), dma((STEPS * B,)), dma((STEPS * B, Y + K)),
        ],
        compiler_params=pltpu.CompilerParams(has_side_effects=True, vmem_limit_bytes=56 * 2**20),
    )(tiles)


def halves(value):
    high = value.astype(BF16)
    return high, (value - high.astype(F32)).astype(BF16)


def dot3(p, q, dims):
    d = functools.partial(lax.dot_general, dimension_numbers=(dims, ((), ())), preferred_element_type=F32)
    return d(p[0], q[0]) + (d(p[0], q[1]) + d(p[1], q[0]))


NT = ((1,), (1,))
NN = ((1,), (0,))


def finish_kernel(R, C, A, B, T, x_ref, m_ref, rs_ref, cs_ref, t_ref, p_ref, mh_ref, ml_ref, qh_ref, ql_ref):
    H = T // LANES
    r, c = lax.axis_index("row"), lax.axis_index("col")
    for n in range(len(LOWER)):
        mh_ref[n], ml_ref[n] = halves(m_ref[n])
    for b in range(B):
        terms = [halves(cs_ref[j, b]) for j in range(STEPS)]
        for k in range(STEPS):
            total = None
            for j in range(k + 1):
                n = SLOT[k, j]
                term = dot3((mh_ref[n], ml_ref[n]), terms[j], NN)
                total = term if total is None else total + term
            qh_ref[k, b], ql_ref[k, b] = halves(total)

    def body(a, carry):
        tile_row = a * R + r
        terms = [halves(rs_ref[j, a]) for j in range(STEPS)]
        panel = []
        for k in range(STEPS):
            total = None
            for j in range(k + 1):
                n = SLOT[k, j]
                term = dot3(terms[j], (mh_ref[n], ml_ref[n]), NT)
                total = term if total is None else total + term
            p_ref[a, k] = jnp.where(tile_row >= k, total, F32(0.0))
            panel.append(halves(total))
        for b in range(B):
            total = load_tile(x_ref, a, b, B, T)
            for k in range(STEPS):
                total = total - dot3(panel[k], (qh_ref[k, b], ql_ref[k, b]), NN)
            keep = (tile_row >= STEPS) & (b * C + c >= STEPS)
            total = jnp.where(keep, total, F32(0.0))
            for h in range(H):
                rows = pl.ds(a * (T * B * H) + b * H + h, T, stride=B * H)
                t_ref[rows, :] = total[:, h * LANES : (h + 1) * LANES]
        return carry

    lax.fori_loop(0, A, body, 0)


def finish(tiles, m, rs, cs, R, C, A, B, T):
    vmem = pl.BlockSpec(memory_space=pltpu.VMEM)
    n = len(LOWER)
    return pl.pallas_call(
        functools.partial(finish_kernel, R, C, A, B, T),
        name="finish",
        out_shape=(jax.ShapeDtypeStruct(tiles.shape, F32), jax.ShapeDtypeStruct((A, STEPS, T, T), F32)),
        in_specs=[vmem] * 4,
        out_specs=(vmem, vmem),
        scratch_shapes=[
            pltpu.VMEM((n, T, T), BF16),
            pltpu.VMEM((n, T, T), BF16),
            pltpu.VMEM((STEPS, B, T, T), BF16),
            pltpu.VMEM((STEPS, B, T, T), BF16),
        ],
        compiler_params=pltpu.CompilerParams(vmem_limit_bytes=56 * 2**20),
    )(tiles, m, rs, cs)


def shards(kernel):
    A, _, T, B, _, _ = kernel.shape
    R, C = lax.axis_size("row"), lax.axis_size("col")
    tiles = kernel.reshape(-1, LANES)
    m, rs, cs = lead(tiles, R, C, A, B, T)
    trailing, panels = finish(tiles, m, rs, cs, R, C, A, B, T)
    return trailing.reshape(kernel.shape), panels.transpose(0, 2, 1, 3).reshape(A, 1, T, STEPS, T)


def solution(mesh):
    in_specs = (P(None, "row", None, None, "col", None),)
    out_specs = (P(None, "row", None, None, "col", None), P(None, "row", None, None, None))
    return jax.shard_map(shards, mesh=mesh, in_specs=in_specs, out_specs=out_specs, check_vma=False)
```

```python
import functools

import jax
import jax.numpy as jnp
from jax import lax
from jax.experimental import pallas as pl
from jax.experimental.pallas import tpu as pltpu
from jax.sharding import PartitionSpec as P

STEPS = 3
PANEL = 16
LANES = 128
LEAD_AT = -1
LEAD_HOP = 2
LEAD_LAG = 4
RS_AT = 0
GAP = 4
HOP = 6
CS_AT = 8
CS_GAP = 3
CS_LAG = 7
PIECES = 2
MESH = pl.DeviceIdType.MESH
F32 = jnp.float32
BF16 = jnp.bfloat16
LOWER = [(i, j) for j in range(STEPS) for i in range(j, STEPS)]
SLOT = {ij: n for n, ij in enumerate(LOWER)}


def split_col(cols):
    width = 1
    while width * width * 4 <= cols:
        width *= 2
    return width, cols // width


def dot_nt(p, q):
    return lax.dot_general(p, q, (((1,), (1,)), ((), ())), precision=lax.Precision.HIGHEST, preferred_element_type=F32)


def dot_nn(p, q):
    return lax.dot_general(p, q, (((1,), (0,)), ((), ())), precision=lax.Precision.HIGHEST, preferred_element_type=F32)


def invert_factor(w_ref, between):
    T = w_ref.shape[0]
    b = PANEL
    lane = lax.broadcasted_iota(jnp.int32, (b, T), 1)
    sub = lax.broadcasted_iota(jnp.int32, (b, T), 0)
    row = lax.broadcasted_iota(jnp.int32, (T, T), 0)
    col = lax.broadcasted_iota(jnp.int32, (T, T), 1)

    wide = T // LANES
    narrow = lax.broadcasted_iota(jnp.int32, (b, LANES), 0)

    def body(p, carry):
        base = pl.multiple_of(p * b, b)
        R = w_ref[pl.ds(base, b), :]
        cols = []
        for j in range(b):
            picked = jnp.sum(jnp.where(lane == base + j, R, F32(0.0)), axis=1, keepdims=True)
            cols.append(jnp.broadcast_to(picked, (b, LANES)))
        V = jnp.where((lane >= base) & (lane < base + b), jnp.where(lane == base + sub, F32(1.0), F32(0.0)), R)
        diag = jnp.ones((b, LANES), F32)
        for j in range(b):
            d = jnp.broadcast_to(cols[j][j : j + 1, :], (b, LANES))
            diag = jnp.where(narrow == j, d, diag)
            if j == b - 1:
                break
            w = jnp.where(narrow > j, cols[j] * (F32(1.0) / d), F32(0.0))
            for i in range(j + 1, b):
                cols[i] = cols[i] - w * cols[i][j : j + 1, :]
            V = V - jnp.concatenate([w] * wide, axis=1) * V[j : j + 1, :]
        V = V * jnp.concatenate([lax.rsqrt(diag)] * wide, axis=1)
        coef = jnp.where(lane >= base + b, V, F32(0.0))
        update = lax.dot_general(
            coef, V, (((0,), (0,)), ((), ())), precision=lax.Precision.HIGHEST, preferred_element_type=F32
        )
        drop = (row >= base + b) & (col >= base) & (col < base + b)
        w_ref[...] = jnp.where(drop, F32(0.0), w_ref[...]) - update
        w_ref[pl.ds(base, b), :] = V
        return carry

    def block(p, carry):
        between(p)
        return body(p, carry)

    lax.fori_loop(0, T // b, block, 0)
    w_ref[...] = jnp.where(row >= col, w_ref[...], F32(0.0))


def read_tile(x_ref, a, b, B, T):
    halves_ = T // LANES
    stride = B * halves_
    start = a * (T * stride) + b * halves_
    return [x_ref[pl.ds(start + h, T, stride=stride), :] for h in range(halves_)]


def load_tile(x_ref, a, b, B, T):
    return jnp.concatenate(read_tile(x_ref, a, b, B, T), axis=1)


def move_tile(dst, x_ref, a, b, B, T):
    for h, value in enumerate(read_tile(x_ref, a, b, B, T)):
        dst[:, h * LANES : (h + 1) * LANES] = value


def lead_kernel(
    R, C, A, B, T, x_ref, m_ref, rs_ref, cs_ref, own_ref, ld_ref, w_ref,
    scat_send, ld_send, ld_sem, ldp_sem, ldc_sem, rs_sem, rs_send, cs_sem, cs_send,
):
    X, Z = split_col(C)
    K = 2 if R % 2 == 0 else 1
    Y = R // K
    r, c = lax.axis_index("row"), lax.axis_index("col")
    z, x = lax.div(c, X), lax.rem(c, X)
    y, core = lax.div(r, K), lax.rem(r, K)
    plane = Y * X
    chunk = T // (R * X)
    items = A * STEPS * PIECES
    tiles = len(LOWER)
    blocks = T // PANEL

    def remote(src, send_sem, recv_sem, dev):
        return pltpu.make_async_remote_copy(
            src_ref=src, dst_ref=src, send_sem=send_sem, recv_sem=recv_sem, device_id=dev, device_id_type=MESH
        )

    def arrived(dst, recv_sem):
        remote(dst, scat_send.at[0, 0], recv_sem, (lax.rem(r + 1, R), c)).wait_recv()

    def near(step, side=0):
        ty, tx = lax.rem(y + step // X, Y), lax.rem(x + step % X, X)
        return ty * K + lax.rem(core + side, K), z * X + tx

    def across(step):
        return lax.rem(y + step, Y) * K + core, c

    def beside(step):
        return y * K + lax.rem(core + step, K), c

    barrier = pltpu.get_barrier_semaphore()
    greeted = [near(step, side) for step in range(plane) for side in range(K) if step or side]
    greeted += [(r, lax.rem(z + step, Z) * X + x) for step in range(1, Z)]
    for dev in greeted:
        pl.semaphore_signal(barrier, inc=1, device_id=dev, device_id_type=MESH)

    def part(ref, row, lane):
        return ref.at[pl.ds(pl.multiple_of((row * X + lane) * chunk, chunk), chunk), :]

    def mine(n):
        return part(ld_ref.at[n], r, x)

    def owner(n):
        i, j = LOWER[n]
        return i % R, j % C

    def scatter(n):
        for step in range(plane):
            for side in range(K):
                if step or side:
                    q, tc = near(step, side)
                    lane = lax.rem(tc, X)
                    yield pltpu.make_async_remote_copy(
                        src_ref=part(own_ref.at[n], q, lane), dst_ref=part(ld_ref.at[n], q, lane),
                        send_sem=scat_send.at[n, step * K + side], recv_sem=ld_sem.at[n],
                        device_id=(q, tc), device_id_type=MESH,
                    )

    for n in range(tiles):
        ri, cj = owner(n)

        @pl.when((r == ri) & (c == cj))
        def _():
            move_tile(own_ref.at[n], x_ref, LOWER[n][0] // R, LOWER[n][1] // C, B, T)
            mine(n)[...] = part(own_ref.at[n], r, x)[...]

    pl.semaphore_wait(barrier, len(greeted))
    for n in range(tiles):
        ri, cj = owner(n)

        @pl.when((r == ri) & (c == cj))
        def _():
            for copy in scatter(n):
                copy.start()

    def lead_out(n):
        zs = owner(n)[1] // X

        def line(m, to):
            return remote(mine(n), ld_send.at[n, m], ld_sem.at[n], (r, to * X + x))

        if n == 0:
            for to in range(Z):
                if to != zs:
                    yield z == zs, line(to, to)
        else:
            yield (z >= zs) & (z + 1 < Z), line(0, lax.rem(z + 1, Z))
            yield (z <= zs) & (z > 0), line(1, lax.rem(z + Z - 1, Z))
        for step in range(1, plane):
            yield r >= 0, remote(mine(n), ld_send.at[n, Z + step], ldp_sem.at[n, step], near(step))
        for side in range(1, K):
            yield r >= 0, remote(mine(n), ld_send.at[n, Z + plane + side], ldc_sem.at[n, side, 0], beside(side))

    def behind(n, step, side=0):
        ty, tx = lax.rem(y + Y - step // X, Y), lax.rem(x + X - step % X, X)
        return part(ld_ref.at[n], ty * K + lax.rem(core + K - side, K), tx)

    def lead_on(n, step):
        for side in range(1, K):
            m = Z + plane + K + (step - 1) * K + side
            yield remote(behind(n, step), ld_send.at[n, m], ldc_sem.at[n, side, step], beside(side))

    def lead_first(n):
        ri, cj = owner(n)
        pl.when((r != ri) | (c != cj))(lambda: arrived(mine(n), ld_sem.at[n]))
        for go, copy in lead_out(n):
            pl.when(go)(copy.start)

    def lead_second(n):
        for step in range(1, plane):
            arrived(behind(n, step), ldp_sem.at[n, step])
            for copy in lead_on(n, step):
                copy.start()

    def lead_third(n):
        for side in range(1, K):
            for step in range(plane):
                arrived(behind(n, step, side), ldc_sem.at[n, side, step])
        w_ref[n] = ld_ref[n]

    def lead_end(n):
        ri, cj = owner(n)

        @pl.when((r == ri) & (c == cj))
        def _():
            for copy in scatter(n):
                copy.wait_send()

        for go, copy in lead_out(n):
            pl.when(go)(copy.wait_send)
        for step in range(1, plane):
            for copy in lead_on(n, step):
                copy.wait_send()

    def item(m):
        tile, piece = lax.div(m, PIECES), lax.rem(m, PIECES)
        k, a = lax.div(tile, A), A - 1 - lax.rem(tile, A)
        source = lax.rem(k, C)
        zs, xs = lax.div(source, X), lax.rem(source, X)
        lane = lax.rem(k + a, X)
        return k, a, piece, source, zs, xs, lane

    def need(m):
        return item(m)[1] * R + r >= STEPS

    def piece_of(m):
        k, a, piece = item(m)[:3]
        rows = T // PIECES
        return rs_ref.at[k, a, pl.ds(pl.multiple_of(piece * rows, rows), rows), :]

    def spread(m):
        _, _, _, source, zs, xs, lane = item(m)
        on = (x == lane) & need(m)
        slot = piece_of(m)

        def copy(n, dev):
            return remote(slot, rs_send.at[m, n], rs_sem.at[m], dev)

        yield (c == source) & (xs != lane) & need(m), copy(0, (r, lax.rem(zs * X + lane, C)))
        yield on & (z >= zs) & (z + 1 < Z), copy(1, (r, lax.rem(c + X, C)))
        yield on & (z <= zs) & (z > 0), copy(2, (r, lax.rem(c + C - X, C)))
        for step in range(1, X):
            other = lax.rem(lane + step, X)
            yield on & jnp.logical_not((z == zs) & (other == xs)), copy(2 + step, (r, z * X + other))

    def forward(m):
        _, _, _, source, _, _, lane = item(m)

        @pl.when(((x == lane) | (c == source)) & need(m))
        def _():
            pl.when(c != source)(lambda: arrived(piece_of(m), rs_sem.at[m]))
            for go, out in spread(m):
                pl.when(go)(out.start)

    def col_at(e):
        k, b = lax.div(e, B), lax.rem(e, B)
        source = lax.rem(k, R)
        return cs_ref.at[k, b], source, lax.div(source, K), lax.rem(source, K)

    def col_out(e):
        slot, source, _, _ = col_at(e)
        for step in range(1, Y):
            yield r == source, remote(slot, cs_send.at[e, step - 1], cs_sem.at[e], across(step))

    def col_on(e):
        slot, _, _, kc = col_at(e)
        for step in range(1, K):
            yield core == kc, remote(slot, cs_send.at[e, Y + step - 2], cs_sem.at[e], beside(step))

    def col_first(e):
        for go, copy in col_out(e):
            pl.when(go)(copy.start)

    def col_second(e):
        slot, source, _, kc = col_at(e)

        @pl.when(core == kc)
        def _():
            pl.when(r != source)(lambda: arrived(slot, cs_sem.at[e]))
            for _, copy in col_on(e):
                copy.start()

    def col_end(e, carry):
        slot, _, _, kc = col_at(e)
        pl.when(core != kc)(lambda: arrived(slot, cs_sem.at[e]))
        for copies in (col_out(e), col_on(e)):
            for go, copy in copies:
                pl.when(go)(copy.wait_send)
        return carry

    cols = STEPS * B
    rounds = A * PIECES

    def rows_work(u):
        for k in range(STEPS):
            source = k % C
            zs, xs = source // X, source % X
            v = u - RS_AT - k * GAP // STEPS - HOP * jnp.abs(z - zs)
            direct = lax.rem(v, GAP) == 0
            v = jnp.where(direct, v, v - HOP)
            h = lax.div(v, GAP)
            turned = lax.rem(k + A - 1 - lax.div(h, PIECES), X) != xs
            turn = jnp.logical_not(direct) & (lax.rem(v, GAP) == 0) & turned & (c != source)

            @pl.when((v >= 0) & (h < rounds) & (turn | (direct & (jnp.logical_not(turned) | (c == source)))))
            def _(k=k, h=h):
                forward(k * rounds + h)

    def lead_work(u):
        for n in range(1, tiles):
            at = LEAD_AT + n + LEAD_HOP * jnp.abs(z - owner(n)[1] // X)
            pl.when(u == at)(functools.partial(lead_first, n))
            pl.when(u == at + LEAD_LAG)(functools.partial(lead_second, n))

    lead_last = LEAD_AT + tiles + LEAD_HOP * (Z - 1) + LEAD_LAG

    def slot_work(u, k):
        if k == 0:
            lead_work(u)
        rows_work(u)
        e, f = u - CS_AT, u - CS_AT - CS_LAG
        pl.when((e >= 0) & (e < cols * CS_GAP) & (lax.rem(e, CS_GAP) == 0))(lambda: col_first(lax.div(e, CS_GAP)))
        pl.when((f >= 0) & (f < cols * CS_GAP) & (lax.rem(f, CS_GAP) == 0))(lambda: col_second(lax.div(f, CS_GAP)))

    lead_first(0)
    for k in range(STEPS):

        def own_rows(a, carry, k=k):
            pl.when(a * R + r >= STEPS)(lambda: move_tile(rs_ref.at[k, a], x_ref, a, k // C, B, T))
            return carry

        @pl.when(c == k % C)
        def _():
            lax.fori_loop(0, A, own_rows, 0)

        for b in range(B):
            pl.when(r == k % R)(lambda: move_tile(cs_ref.at[k, b], x_ref, k // R, b, B, T))
    lax.fori_loop(RS_AT, 0, lambda u, s: (rows_work(u), s)[1], 0)
    lead_second(0)
    lead_third(0)
    for k in range(STEPS):
        invert_factor(w_ref.at[SLOT[k, k]], lambda p, k=k: slot_work(k * blocks + p, k))
        inv = w_ref[SLOT[k, k]]
        if k == 0:
            if lead_last > blocks:
                lax.fori_loop(blocks, lead_last, lambda u, s: (lead_work(u), s)[1], 0)
            for n in range(1, tiles):
                lead_third(n)
            for i in range(STEPS):

                @pl.when(r == i % R)
                def _():
                    for j in range(STEPS):
                        rs_ref[j, i // R] = ld_ref[SLOT[i, j]] if j <= i else jnp.zeros((T, T), F32)

        for i in range(k + 1, STEPS):
            w_ref[SLOT[i, k]] = dot_nt(w_ref[SLOT[i, k]], inv)
        for j in range(k + 1, STEPS):
            for i in range(j, STEPS):
                w_ref[SLOT[i, j]] = w_ref[SLOT[i, j]] - dot_nt(w_ref[SLOT[i, k]], w_ref[SLOT[j, k]])
    for k in range(STEPS):
        m_ref[SLOT[k, k]] = w_ref[SLOT[k, k]]
        for i in range(k + 1, STEPS):
            total = dot_nn(w_ref[SLOT[i, k]], m_ref[SLOT[k, k]])
            for j in range(k + 1, i):
                total = total + dot_nn(w_ref[SLOT[i, j]], m_ref[SLOT[j, k]])
            m_ref[SLOT[i, k]] = -dot_nn(w_ref[SLOT[i, i]], total)

    last = RS_AT + GAP * rounds + HOP * Z
    last = max(last, CS_AT + CS_LAG + cols * CS_GAP)
    lax.fori_loop(STEPS * blocks, max(last, STEPS * blocks), lambda u, s: (slot_work(u, STEPS), s)[1], 0)

    def finish_item(m, carry):
        _, _, _, source, _, _, lane = item(m)
        pl.when((x != lane) & (c != source) & need(m))(lambda: arrived(piece_of(m), rs_sem.at[m]))
        for go, out in spread(m):
            pl.when(go)(out.wait_send)
        return carry

    lax.fori_loop(0, items, finish_item, 0)
    lax.fori_loop(0, cols, col_end, 0)
    for n in range(tiles):
        lead_end(n)


def lead(tiles, R, C, A, B, T):
    X, Z = split_col(C)
    K = 2 if R % 2 == 0 else 1
    Y = R // K
    plane = X * Y
    n = len(LOWER)
    items = STEPS * A * PIECES
    vmem = pl.BlockSpec(memory_space=pltpu.VMEM)
    dma = pltpu.SemaphoreType.DMA
    return pl.pallas_call(
        functools.partial(lead_kernel, R, C, A, B, T),
        name="lead",
        out_shape=(
            jax.ShapeDtypeStruct((n, T, T), F32),
            jax.ShapeDtypeStruct((STEPS, A, T, T), F32),
            jax.ShapeDtypeStruct((STEPS, B, T, T), F32),
        ),
        in_specs=[vmem],
        out_specs=(vmem, vmem, vmem),
        scratch_shapes=[
            pltpu.VMEM((n, T, T), F32),
            pltpu.VMEM((n, T, T), F32),
            pltpu.VMEM((n, T, T), F32),
            dma((n, plane * K)), dma((n, Z + plane + K + plane * K)), dma((n,)), dma((n, plane)), dma((n, K, plane)),
            dma((items,)), dma((items, X + 2)), dma((STEPS * B,)), dma((STEPS * B, Y + K)),
        ],
        compiler_params=pltpu.CompilerParams(has_side_effects=True, collective_id=0, vmem_limit_bytes=56 * 2**20),
    )(tiles)


def halves(value):
    high = value.astype(BF16)
    return high, (value - high.astype(F32)).astype(BF16)


def dot3(p, q, dims):
    d = functools.partial(lax.dot_general, dimension_numbers=(dims, ((), ())), preferred_element_type=F32)
    return d(p[0], q[0]) + (d(p[0], q[1]) + d(p[1], q[0]))


NT = ((1,), (1,))
NN = ((1,), (0,))


def finish_kernel(R, C, A, B, T, x_ref, m_ref, rs_ref, cs_ref, t_ref, p_ref, mh_ref, ml_ref, qh_ref, ql_ref):
    H = T // LANES
    r, c = lax.axis_index("row"), lax.axis_index("col")
    for n in range(len(LOWER)):
        mh_ref[n], ml_ref[n] = halves(m_ref[n])
    for b in range(B):
        terms = [halves(cs_ref[j, b]) for j in range(STEPS)]
        for k in range(STEPS):
            total = None
            for j in range(k + 1):
                n = SLOT[k, j]
                term = dot3((mh_ref[n], ml_ref[n]), terms[j], NN)
                total = term if total is None else total + term
            qh_ref[k, b], ql_ref[k, b] = halves(total)

    def body(a, carry):
        tile_row = a * R + r
        terms = [halves(rs_ref[j, a]) for j in range(STEPS)]
        panel = []
        for k in range(STEPS):
            total = None
            for j in range(k + 1):
                n = SLOT[k, j]
                term = dot3(terms[j], (mh_ref[n], ml_ref[n]), NT)
                total = term if total is None else total + term
            p_ref[a, k] = jnp.where(tile_row >= k, total, F32(0.0))
            panel.append(halves(total))
        for b in range(B):
            total = load_tile(x_ref, a, b, B, T)
            for k in range(STEPS):
                total = total - dot3(panel[k], (qh_ref[k, b], ql_ref[k, b]), NN)
            keep = (tile_row >= STEPS) & (b * C + c >= STEPS)
            total = jnp.where(keep, total, F32(0.0))
            for h in range(H):
                rows = pl.ds(a * (T * B * H) + b * H + h, T, stride=B * H)
                t_ref[rows, :] = total[:, h * LANES : (h + 1) * LANES]
        return carry

    lax.fori_loop(0, A, body, 0)


def finish(tiles, m, rs, cs, R, C, A, B, T):
    vmem = pl.BlockSpec(memory_space=pltpu.VMEM)
    n = len(LOWER)
    return pl.pallas_call(
        functools.partial(finish_kernel, R, C, A, B, T),
        name="finish",
        out_shape=(jax.ShapeDtypeStruct(tiles.shape, F32), jax.ShapeDtypeStruct((A, STEPS, T, T), F32)),
        in_specs=[vmem] * 4,
        out_specs=(vmem, vmem),
        scratch_shapes=[
            pltpu.VMEM((n, T, T), BF16),
            pltpu.VMEM((n, T, T), BF16),
            pltpu.VMEM((STEPS, B, T, T), BF16),
            pltpu.VMEM((STEPS, B, T, T), BF16),
        ],
        compiler_params=pltpu.CompilerParams(vmem_limit_bytes=56 * 2**20),
    )(tiles, m, rs, cs)


def shards(kernel):
    A, _, T, B, _, _ = kernel.shape
    R, C = lax.axis_size("row"), lax.axis_size("col")
    tiles = kernel.reshape(-1, LANES)
    m, rs, cs = lead(tiles, R, C, A, B, T)
    trailing, panels = finish(tiles, m, rs, cs, R, C, A, B, T)
    return trailing.reshape(kernel.shape), panels.transpose(0, 2, 1, 3).reshape(A, 1, T, STEPS, T)


def solution(mesh):
    in_specs = (P(None, "row", None, None, "col", None),)
    out_specs = (P(None, "row", None, None, "col", None), P(None, "row", None, None, None))
    return jax.shard_map(shards, mesh=mesh, in_specs=in_specs, out_specs=out_specs, check_vma=False)
```

```python
import functools

import jax
import jax.numpy as jnp
from jax import lax
from jax.experimental import pallas as pl
from jax.experimental.pallas import tpu as pltpu
from jax.sharding import PartitionSpec as P

STEPS = 3
PANEL = 16
LANES = 128
GROUPS = 4
LEAD_AT = 2
RS_AT = -9
GAP = 4
HOP = 9
CS_AT = 8
CS_GAP = 3
CS_LAG = 7
PIECES = 2
MESH = pl.DeviceIdType.MESH
F32 = jnp.float32
BF16 = jnp.bfloat16
LOWER = [(i, j) for j in range(STEPS) for i in range(j, STEPS)]
SLOT = {ij: n for n, ij in enumerate(LOWER)}


def split_col(cols):
    width = 1
    while width * width * 4 <= cols:
        width *= 2
    return width, cols // width


def dot_nt(p, q):
    return lax.dot_general(p, q, (((1,), (1,)), ((), ())), precision=lax.Precision.HIGHEST, preferred_element_type=F32)


def dot_nn(p, q):
    return lax.dot_general(p, q, (((1,), (0,)), ((), ())), precision=lax.Precision.HIGHEST, preferred_element_type=F32)


def invert_factor(w_ref, between):
    T = w_ref.shape[0]
    b, half = PANEL, PANEL // 2
    lane = lax.broadcasted_iota(jnp.int32, (b, T), 1)
    sub = lax.broadcasted_iota(jnp.int32, (b, T), 0)
    row = lax.broadcasted_iota(jnp.int32, (T, T), 0)
    col = lax.broadcasted_iota(jnp.int32, (T, T), 1)
    wide = T // LANES
    narrow = lax.broadcasted_iota(jnp.int32, (half, LANES), 0)
    zero = F32(0.0)

    def spread(value):
        return jnp.concatenate([value] * wide, axis=1)

    def body(p, first):
        base = pl.multiple_of(p * b, b)
        R = w_ref[pl.ds(base, b), :]
        cols = []
        for j in range(b):
            picked = jnp.sum(jnp.where(lane == base + j, R, zero), axis=1, keepdims=True)
            cols.append([jnp.broadcast_to(picked[h * half : (h + 1) * half], (half, LANES)) for h in range(2)])
        V = jnp.where((lane >= base) & (lane < base + b), jnp.where(lane == base + sub, F32(1.0), zero), R)
        V = [V[:half], V[half:]]
        diag = [jnp.ones((half, LANES), F32) for _ in range(2)]
        for j in range(b):
            own, at = divmod(j, half)
            d = jnp.broadcast_to(cols[j][own][at : at + 1, :], (half, LANES))
            diag[own] = jnp.where(narrow == at, d, diag[own])
            if j == b - 1:
                break
            inverse = F32(1.0) / d
            pivot = V[own][at : at + 1, :]
            for h in range(own, 2):
                w = cols[j][h] * inverse
                if h == own:
                    w = jnp.where(narrow > at, w, zero)
                V[h] = V[h] - spread(w) * pivot
                for i in range(j + 1, b):
                    cols[i][h] = cols[i][h] - w * cols[i][own][at : at + 1, :] if h > own else cols[i][h]
            w = jnp.where(narrow > at, cols[j][own] * inverse, zero)
            for i in range(j + 1, b):
                cols[i][own] = cols[i][own] - w * cols[i][own][at : at + 1, :]
        V = jnp.concatenate([v * spread(lax.rsqrt(d)) for v, d in zip(V, diag)], axis=0)
        coef = jnp.where(lane >= base + b, V, zero)
        update = lax.dot_general(
            coef[:, first:], V, (((0,), (0,)), ((), ())), precision=lax.Precision.HIGHEST, preferred_element_type=F32
        )
        drop = (row[first:] >= base + b) & (col[first:] >= base) & (col[first:] < base + b)
        w_ref[first:, :] = jnp.where(drop, zero, w_ref[first:, :]) - update
        w_ref[pl.ds(base, b), :] = V

    step = T // GROUPS

    for g in range(GROUPS):

        def block(p, carry, first=g * step):
            between(p)
            body(p, first)
            return carry

        lax.fori_loop(g * step // b, (g + 1) * step // b, block, 0)
    w_ref[...] = jnp.where(row >= col, w_ref[...], zero)


def read_tile(x_ref, a, b, B, T):
    halves_ = T // LANES
    stride = B * halves_
    start = a * (T * stride) + b * halves_
    return [x_ref[pl.ds(start + h, T, stride=stride), :] for h in range(halves_)]


def load_tile(x_ref, a, b, B, T):
    return jnp.concatenate(read_tile(x_ref, a, b, B, T), axis=1)


def move_tile(dst, x_ref, a, b, B, T):
    for h, value in enumerate(read_tile(x_ref, a, b, B, T)):
        dst[:, h * LANES : (h + 1) * LANES] = value


def lead_kernel(
    R, C, A, B, T, x_ref, m_ref, rs_ref, cs_ref, own_ref, ld_ref, w_ref,
    scat_send, ld_send, ld_sem, ldp_sem, ldc_sem, rs_sem, rs_send, cs_sem, cs_send,
):
    X, Z = split_col(C)
    K = 2 if R % 2 == 0 else 1
    Y = R // K
    r, c = lax.axis_index("row"), lax.axis_index("col")
    z, x = lax.div(c, X), lax.rem(c, X)
    y, core = lax.div(r, K), lax.rem(r, K)
    plane = Y * X
    chunk = T // (R * X)
    items = A * STEPS * PIECES
    tiles = len(LOWER)
    blocks = T // PANEL

    def remote(src, send_sem, recv_sem, dev):
        return pltpu.make_async_remote_copy(
            src_ref=src, dst_ref=src, send_sem=send_sem, recv_sem=recv_sem, device_id=dev, device_id_type=MESH
        )

    def arrived(dst, recv_sem):
        remote(dst, scat_send.at[0, 0], recv_sem, (lax.rem(r + 1, R), c)).wait_recv()

    def near(step, side=0):
        ty, tx = lax.rem(y + step // X, Y), lax.rem(x + step % X, X)
        return ty * K + lax.rem(core + side, K), z * X + tx

    def across(step):
        return lax.rem(y + step, Y) * K + core, c

    def beside(step):
        return y * K + lax.rem(core + step, K), c

    barrier = pltpu.get_barrier_semaphore()
    greeted = [near(step, side) for step in range(plane) for side in range(K) if step or side]
    greeted += [(r, lax.rem(z + step, Z) * X + x) for step in range(1, Z)]
    for dev in greeted:
        pl.semaphore_signal(barrier, inc=1, device_id=dev, device_id_type=MESH)

    def part(ref, row, lane):
        return ref.at[pl.ds(pl.multiple_of((row * X + lane) * chunk, chunk), chunk), :]

    def mine(n):
        return part(ld_ref.at[n], r, x)

    def owner(n):
        i, j = LOWER[n]
        return i % R, j % C

    def scatter(n):
        for step in range(plane):
            for side in range(K):
                if step or side:
                    q, tc = near(step, side)
                    lane = lax.rem(tc, X)
                    yield pltpu.make_async_remote_copy(
                        src_ref=part(own_ref.at[n], q, lane), dst_ref=part(ld_ref.at[n], q, lane),
                        send_sem=scat_send.at[n, step * K + side], recv_sem=ld_sem.at[n],
                        device_id=(q, tc), device_id_type=MESH,
                    )

    for n in range(tiles):
        ri, cj = owner(n)

        @pl.when((r == ri) & (c == cj))
        def _():
            move_tile(own_ref.at[n], x_ref, LOWER[n][0] // R, LOWER[n][1] // C, B, T)
            mine(n)[...] = part(own_ref.at[n], r, x)[...]

    pl.semaphore_wait(barrier, len(greeted))
    for n in range(tiles):
        ri, cj = owner(n)

        @pl.when((r == ri) & (c == cj))
        def _():
            for copy in scatter(n):
                copy.start()

    def lead_out(n):
        zs = owner(n)[1] // X

        def line(m, to):
            return remote(mine(n), ld_send.at[n, m], ld_sem.at[n], (r, to * X + x))

        if n == 0:
            for to in range(Z):
                if to != zs:
                    yield z == zs, line(to, to)
        else:
            yield (z >= zs) & (z + 1 < Z), line(0, lax.rem(z + 1, Z))
            yield (z <= zs) & (z > 0), line(1, lax.rem(z + Z - 1, Z))
        for step in range(1, plane):
            yield r >= 0, remote(mine(n), ld_send.at[n, Z + step], ldp_sem.at[n, step], near(step))
        for side in range(1, K):
            yield r >= 0, remote(mine(n), ld_send.at[n, Z + plane + side], ldc_sem.at[n, side, 0], beside(side))

    def behind(n, step, side=0):
        ty, tx = lax.rem(y + Y - step // X, Y), lax.rem(x + X - step % X, X)
        return part(ld_ref.at[n], ty * K + lax.rem(core + K - side, K), tx)

    def lead_on(n, step):
        for side in range(1, K):
            m = Z + plane + K + (step - 1) * K + side
            yield remote(behind(n, step), ld_send.at[n, m], ldc_sem.at[n, side, step], beside(side))

    def lead_first(n):
        ri, cj = owner(n)
        pl.when((r != ri) | (c != cj))(lambda: arrived(mine(n), ld_sem.at[n]))
        for go, copy in lead_out(n):
            pl.when(go)(copy.start)

    def lead_second(n):
        for step in range(1, plane):
            arrived(behind(n, step), ldp_sem.at[n, step])
            for copy in lead_on(n, step):
                copy.start()

    def lead_third(n):
        for side in range(1, K):
            for step in range(plane):
                arrived(behind(n, step, side), ldc_sem.at[n, side, step])
        w_ref[n] = ld_ref[n]

    def lead_end(n):
        ri, cj = owner(n)

        @pl.when((r == ri) & (c == cj))
        def _():
            for copy in scatter(n):
                copy.wait_send()

        for go, copy in lead_out(n):
            pl.when(go)(copy.wait_send)
        for step in range(1, plane):
            for copy in lead_on(n, step):
                copy.wait_send()

    def item(m):
        tile, piece = lax.div(m, PIECES), lax.rem(m, PIECES)
        k, a = lax.div(tile, A), A - 1 - lax.rem(tile, A)
        source = lax.rem(k, C)
        zs, xs = lax.div(source, X), lax.rem(source, X)
        lane = lax.rem(k + a, X)
        return k, a, piece, source, zs, xs, lane

    def need(m):
        return item(m)[1] * R + r >= STEPS

    def piece_of(m):
        k, a, piece = item(m)[:3]
        rows = T // PIECES
        return rs_ref.at[k, a, pl.ds(pl.multiple_of(piece * rows, rows), rows), :]

    def spread(m):
        _, _, _, source, zs, xs, lane = item(m)
        on = (x == lane) & need(m)
        slot = piece_of(m)

        def copy(n, dev):
            return remote(slot, rs_send.at[m, n], rs_sem.at[m], dev)

        yield (c == source) & (xs != lane) & need(m), copy(0, (r, lax.rem(zs * X + lane, C)))
        yield on & (z >= zs) & (z + 1 < Z), copy(1, (r, lax.rem(c + X, C)))
        yield on & (z <= zs) & (z > 0), copy(2, (r, lax.rem(c + C - X, C)))
        for step in range(1, X):
            other = lax.rem(lane + step, X)
            yield on & jnp.logical_not((z == zs) & (other == xs)), copy(2 + step, (r, z * X + other))

    def forward(m):
        _, _, _, source, _, _, lane = item(m)

        @pl.when(((x == lane) | (c == source)) & need(m))
        def _():
            pl.when(c != source)(lambda: arrived(piece_of(m), rs_sem.at[m]))
            for go, out in spread(m):
                pl.when(go)(out.start)

    def col_at(e):
        k, b = lax.div(e, B), lax.rem(e, B)
        source = lax.rem(k, R)
        return cs_ref.at[k, b], source, lax.div(source, K), lax.rem(source, K)

    def col_out(e):
        slot, source, _, _ = col_at(e)
        for step in range(1, Y):
            yield r == source, remote(slot, cs_send.at[e, step - 1], cs_sem.at[e], across(step))

    def col_on(e):
        slot, _, _, kc = col_at(e)
        for step in range(1, K):
            yield core == kc, remote(slot, cs_send.at[e, Y + step - 2], cs_sem.at[e], beside(step))

    def col_first(e):
        for go, copy in col_out(e):
            pl.when(go)(copy.start)

    def col_second(e):
        slot, source, _, kc = col_at(e)

        @pl.when(core == kc)
        def _():
            pl.when(r != source)(lambda: arrived(slot, cs_sem.at[e]))
            for _, copy in col_on(e):
                copy.start()

    def col_end(e, carry):
        slot, _, _, kc = col_at(e)
        pl.when(core != kc)(lambda: arrived(slot, cs_sem.at[e]))
        for copies in (col_out(e), col_on(e)):
            for go, copy in copies:
                pl.when(go)(copy.wait_send)
        return carry

    cols = STEPS * B
    rounds = A * PIECES

    def rows_work(u):
        for k in range(STEPS):
            source = k % C
            zs, xs = source // X, source % X
            v = u - RS_AT - k * GAP // STEPS - HOP * jnp.abs(z - zs)
            direct = lax.rem(v, GAP) == 0
            v = jnp.where(direct, v, v - HOP)
            h = lax.div(v, GAP)
            turned = lax.rem(k + A - 1 - lax.div(h, PIECES), X) != xs
            turn = jnp.logical_not(direct) & (lax.rem(v, GAP) == 0) & turned

            @pl.when((v >= 0) & (h < rounds) & (c != source) & (turn | (direct & jnp.logical_not(turned))))
            def _(k=k, h=h):
                forward(k * rounds + h)

    def lead_work(u):
        for n in range(1, tiles):
            pl.when(u == LEAD_AT + n)(functools.partial(lead_second, n))

    def slot_work(u, k):
        if k == 0:
            lead_work(u)
        rows_work(u)
        e, f = u - CS_AT, u - CS_AT - CS_LAG
        pl.when((e >= 0) & (e < cols * CS_GAP) & (lax.rem(e, CS_GAP) == 0))(lambda: col_first(lax.div(e, CS_GAP)))
        pl.when((f >= 0) & (f < cols * CS_GAP) & (lax.rem(f, CS_GAP) == 0))(lambda: col_second(lax.div(f, CS_GAP)))

    lead_first(0)
    for k in range(STEPS):

        def own_rows(a, carry, k=k):
            pl.when(a * R + r >= STEPS)(lambda: move_tile(rs_ref.at[k, a], x_ref, a, k // C, B, T))
            return carry

        @pl.when(c == k % C)
        def _():
            lax.fori_loop(0, A, own_rows, 0)

        for b in range(B):
            pl.when(r == k % R)(lambda: move_tile(cs_ref.at[k, b], x_ref, k // R, b, B, T))
    for n in range(1, tiles):
        lead_first(n)
    for k in range(STEPS):

        @pl.when(c == k % C)
        def _(k=k):
            lax.fori_loop(0, rounds, lambda h, s: (forward(k * rounds + h), s)[1], 0)

    lead_second(0)
    lead_third(0)
    for k in range(STEPS):
        invert_factor(w_ref.at[SLOT[k, k]], lambda p, k=k: slot_work(k * blocks + p, k))
        inv = w_ref[SLOT[k, k]]
        if k == 0:
            for n in range(1, tiles):
                lead_third(n)
            for i in range(STEPS):

                @pl.when(r == i % R)
                def _():
                    for j in range(STEPS):
                        rs_ref[j, i // R] = ld_ref[SLOT[i, j]] if j <= i else jnp.zeros((T, T), F32)

        for i in range(k + 1, STEPS):
            w_ref[SLOT[i, k]] = dot_nt(w_ref[SLOT[i, k]], inv)
        for j in range(k + 1, STEPS):
            for i in range(j, STEPS):
                w_ref[SLOT[i, j]] = w_ref[SLOT[i, j]] - dot_nt(w_ref[SLOT[i, k]], w_ref[SLOT[j, k]])
    for k in range(STEPS):
        m_ref[SLOT[k, k]] = w_ref[SLOT[k, k]]
        for i in range(k + 1, STEPS):
            total = dot_nn(w_ref[SLOT[i, k]], m_ref[SLOT[k, k]])
            for j in range(k + 1, i):
                total = total + dot_nn(w_ref[SLOT[i, j]], m_ref[SLOT[j, k]])
            m_ref[SLOT[i, k]] = -dot_nn(w_ref[SLOT[i, i]], total)

    last = RS_AT + GAP * (rounds + 1) + HOP * Z
    last = max(last, CS_AT + CS_LAG + cols * CS_GAP)
    lax.fori_loop(STEPS * blocks, max(last, STEPS * blocks), lambda u, s: (slot_work(u, STEPS), s)[1], 0)

    def finish_item(m, carry):
        _, _, _, source, _, _, lane = item(m)
        pl.when((x != lane) & (c != source) & need(m))(lambda: arrived(piece_of(m), rs_sem.at[m]))
        for go, out in spread(m):
            pl.when(go)(out.wait_send)
        return carry

    lax.fori_loop(0, items, finish_item, 0)
    lax.fori_loop(0, cols, col_end, 0)
    for n in range(tiles):
        lead_end(n)


def lead(tiles, R, C, A, B, T):
    X, Z = split_col(C)
    K = 2 if R % 2 == 0 else 1
    Y = R // K
    plane = X * Y
    n = len(LOWER)
    items = STEPS * A * PIECES
    vmem = pl.BlockSpec(memory_space=pltpu.VMEM)
    dma = pltpu.SemaphoreType.DMA
    return pl.pallas_call(
        functools.partial(lead_kernel, R, C, A, B, T),
        name="lead",
        out_shape=(
            jax.ShapeDtypeStruct((n, T, T), F32),
            jax.ShapeDtypeStruct((STEPS, A, T, T), F32),
            jax.ShapeDtypeStruct((STEPS, B, T, T), F32),
        ),
        in_specs=[vmem],
        out_specs=(vmem, vmem, vmem),
        scratch_shapes=[
            pltpu.VMEM((n, T, T), F32),
            pltpu.VMEM((n, T, T), F32),
            pltpu.VMEM((n, T, T), F32),
            dma((n, plane * K)), dma((n, Z + plane + K + plane * K)), dma((n,)), dma((n, plane)), dma((n, K, plane)),
            dma((items,)), dma((items, X + 2)), dma((STEPS * B,)), dma((STEPS * B, Y + K)),
        ],
        compiler_params=pltpu.CompilerParams(has_side_effects=True, collective_id=0, vmem_limit_bytes=56 * 2**20),
    )(tiles)


def halves(value):
    high = value.astype(BF16)
    return high, (value - high.astype(F32)).astype(BF16)


def dot3(p, q, dims):
    d = functools.partial(lax.dot_general, dimension_numbers=(dims, ((), ())), preferred_element_type=F32)
    return d(p[0], q[0]) + (d(p[0], q[1]) + d(p[1], q[0]))


NT = ((1,), (1,))
NN = ((1,), (0,))


def finish_kernel(R, C, A, B, T, x_ref, m_ref, rs_ref, cs_ref, t_ref, p_ref, mh_ref, ml_ref, qh_ref, ql_ref):
    H = T // LANES
    r, c = lax.axis_index("row"), lax.axis_index("col")
    a = pl.program_id(0)

    @pl.when(a == 0)
    def _():
        for n in range(len(LOWER)):
            mh_ref[n], ml_ref[n] = halves(m_ref[n])
        for b in range(B):
            terms = [halves(cs_ref[j, b]) for j in range(STEPS)]
            for k in range(STEPS):
                total = None
                for j in range(k + 1):
                    n = SLOT[k, j]
                    term = dot3((mh_ref[n], ml_ref[n]), terms[j], NN)
                    total = term if total is None else total + term
                qh_ref[k, b], ql_ref[k, b] = halves(total)

    tile_row = a * R + r
    terms = [halves(rs_ref[j, 0]) for j in range(STEPS)]
    panel = []
    for k in range(STEPS):
        total = None
        for j in range(k + 1):
            n = SLOT[k, j]
            term = dot3(terms[j], (mh_ref[n], ml_ref[n]), NT)
            total = term if total is None else total + term
        p_ref[0, k] = jnp.where(tile_row >= k, total, F32(0.0))
        panel.append(halves(total))
    for b in range(B):
        total = load_tile(x_ref, 0, b, B, T)
        for k in range(STEPS):
            total = total - dot3(panel[k], (qh_ref[k, b], ql_ref[k, b]), NN)
        keep = (tile_row >= STEPS) & (b * C + c >= STEPS)
        total = jnp.where(keep, total, F32(0.0))
        for h in range(H):
            t_ref[pl.ds(b * H + h, T, stride=B * H), :] = total[:, h * LANES : (h + 1) * LANES]


def finish(tiles, m, rs, cs, R, C, A, B, T):
    n = len(LOWER)
    rows = tiles.shape[0] // A
    flat = pl.BlockSpec((rows, LANES), lambda a: (a, 0))
    return pl.pallas_call(
        functools.partial(finish_kernel, R, C, A, B, T),
        name="finish",
        grid=(A,),
        out_shape=(jax.ShapeDtypeStruct(tiles.shape, F32), jax.ShapeDtypeStruct((A, STEPS, T, T), F32)),
        in_specs=[
            flat,
            pl.BlockSpec((n, T, T), lambda a: (0, 0, 0)),
            pl.BlockSpec((STEPS, 1, T, T), lambda a: (0, a, 0, 0)),
            pl.BlockSpec((STEPS, B, T, T), lambda a: (0, 0, 0, 0)),
        ],
        out_specs=(flat, pl.BlockSpec((1, STEPS, T, T), lambda a: (a, 0, 0, 0))),
        scratch_shapes=[
            pltpu.VMEM((n, T, T), BF16),
            pltpu.VMEM((n, T, T), BF16),
            pltpu.VMEM((STEPS, B, T, T), BF16),
            pltpu.VMEM((STEPS, B, T, T), BF16),
        ],
        compiler_params=pltpu.CompilerParams(vmem_limit_bytes=56 * 2**20),
    )(tiles, m, rs, cs)


def shards(kernel):
    A, _, T, B, _, _ = kernel.shape
    R, C = lax.axis_size("row"), lax.axis_size("col")
    tiles = kernel.reshape(-1, LANES)
    m, rs, cs = lead(tiles, R, C, A, B, T)
    trailing, panels = finish(tiles, m, rs, cs, R, C, A, B, T)
    return trailing.reshape(kernel.shape), panels.transpose(0, 2, 1, 3).reshape(A, 1, T, STEPS, T)


def solution(mesh):
    in_specs = (P(None, "row", None, None, "col", None),)
    out_specs = (P(None, "row", None, None, "col", None), P(None, "row", None, None, None))
    return jax.shard_map(shards, mesh=mesh, in_specs=in_specs, out_specs=out_specs, check_vma=False)
```

```python
import functools

import jax
import jax.numpy as jnp
from jax import lax
from jax.experimental import pallas as pl
from jax.experimental.pallas import tpu as pltpu
from jax.sharding import PartitionSpec as P

STEPS = 3
PANEL = 16
LANES = 128
GROUPS = 4
EVERY = 2
LATE = 2
RS_AT = -5
GAP = 2
HOP = 5
CS_AT = 4
CS_GAP = 2
CS_LAG = 4
PIECES = 2
MESH = pl.DeviceIdType.MESH
F32 = jnp.float32
BF16 = jnp.bfloat16
LOWER = [(i, j) for j in range(STEPS) for i in range(j, STEPS)]
SLOT = {ij: n for n, ij in enumerate(LOWER)}


def split_col(cols):
    width = 1
    while width * width * 4 <= cols:
        width *= 2
    return width, cols // width


def dot_nt(p, q):
    return lax.dot_general(p, q, (((1,), (1,)), ((), ())), precision=lax.Precision.HIGHEST, preferred_element_type=F32)


def invert_factor(w_ref, between):
    T = w_ref.shape[0]
    b, half = PANEL, PANEL // 2
    lane = lax.broadcasted_iota(jnp.int32, (b, T), 1)
    sub = lax.broadcasted_iota(jnp.int32, (b, T), 0)
    row = lax.broadcasted_iota(jnp.int32, (T, T), 0)
    col = lax.broadcasted_iota(jnp.int32, (T, T), 1)
    wide = T // LANES
    narrow = lax.broadcasted_iota(jnp.int32, (half, LANES), 0)
    zero = F32(0.0)

    def spread(value):
        return jnp.concatenate([value] * wide, axis=1)

    def body(p, first):
        base = pl.multiple_of(p * b, b)
        R = w_ref[pl.ds(base, b), :]
        cols = []
        for j in range(b):
            picked = jnp.sum(jnp.where(lane == base + j, R, zero), axis=1, keepdims=True)
            cols.append([jnp.broadcast_to(picked[h * half : (h + 1) * half], (half, LANES)) for h in range(2)])
        V = jnp.where((lane >= base) & (lane < base + b), jnp.where(lane == base + sub, F32(1.0), zero), R)
        V = [V[:half], V[half:]]
        diag = [jnp.ones((half, LANES), F32) for _ in range(2)]
        for j in range(b):
            own, at = divmod(j, half)
            d = jnp.broadcast_to(cols[j][own][at : at + 1, :], (half, LANES))
            diag[own] = jnp.where(narrow == at, d, diag[own])
            if j == b - 1:
                break
            inverse = F32(1.0) / d
            pivot = V[own][at : at + 1, :]
            for h in range(own, 2):
                w = cols[j][h] * inverse
                if h == own:
                    w = jnp.where(narrow > at, w, zero)
                V[h] = V[h] - spread(w) * pivot
                for i in range(j + 1, b):
                    cols[i][h] = cols[i][h] - w * cols[i][own][at : at + 1, :] if h > own else cols[i][h]
            w = jnp.where(narrow > at, cols[j][own] * inverse, zero)
            for i in range(j + 1, b):
                cols[i][own] = cols[i][own] - w * cols[i][own][at : at + 1, :]
        V = jnp.concatenate([v * spread(lax.rsqrt(d)) for v, d in zip(V, diag)], axis=0)
        coef = jnp.where(lane >= base + b, V, zero)
        update = lax.dot_general(
            coef[:, first:], V, (((0,), (0,)), ((), ())), precision=lax.Precision.HIGHEST, preferred_element_type=F32
        )
        drop = (row[first:] >= base + b) & (col[first:] >= base) & (col[first:] < base + b)
        w_ref[first:, :] = jnp.where(drop, zero, w_ref[first:, :]) - update
        w_ref[pl.ds(base, b), :] = V

    step = T // GROUPS

    for g in range(GROUPS):

        def block(q, carry, first=g * step):
            between(q)
            for p in range(EVERY):
                body(q * EVERY + p, first)
            return carry

        lax.fori_loop(g * step // b // EVERY, (g + 1) * step // b // EVERY, block, 0)
    w_ref[...] = jnp.where(row >= col, w_ref[...], zero)


def read_tile(x_ref, a, b, B, T):
    halves_ = T // LANES
    stride = B * halves_
    start = a * (T * stride) + b * halves_
    return [x_ref[pl.ds(start + h, T, stride=stride), :] for h in range(halves_)]


def load_tile(x_ref, a, b, B, T):
    return jnp.concatenate(read_tile(x_ref, a, b, B, T), axis=1)


def move_tile(dst, x_ref, a, b, B, T):
    for h, value in enumerate(read_tile(x_ref, a, b, B, T)):
        dst[:, h * LANES : (h + 1) * LANES] = value


def lead_kernel(
    R, C, A, B, T, x_ref, m_out, rs_out, cs_out, m_ref, rs_ref, cs_ref, own_ref, ld_ref, w_ref, m_sem, out_sem, col_sem,
    scat_send, ld_send, ld_sem, ldp_sem, ldc_sem, rs_sem, rs_send, cs_sem, cs_send,
):
    X, Z = split_col(C)
    K = 2 if R % 2 == 0 else 1
    Y = R // K
    r, c = lax.axis_index("row"), lax.axis_index("col")
    z, x = lax.div(c, X), lax.rem(c, X)
    y, core = lax.div(r, K), lax.rem(r, K)
    plane = Y * X
    chunk = T // (R * X)
    items = A * STEPS * PIECES
    tiles = len(LOWER)
    blocks = T // PANEL // EVERY

    def remote(src, send_sem, recv_sem, dev):
        return pltpu.make_async_remote_copy(
            src_ref=src, dst_ref=src, send_sem=send_sem, recv_sem=recv_sem, device_id=dev, device_id_type=MESH
        )

    def arrived(dst, recv_sem):
        remote(dst, scat_send.at[0, 0], recv_sem, (lax.rem(r + 1, R), c)).wait_recv()

    def near(step, side=0):
        ty, tx = lax.rem(y + step // X, Y), lax.rem(x + step % X, X)
        return ty * K + lax.rem(core + side, K), z * X + tx

    def across(step):
        return lax.rem(y + step, Y) * K + core, c

    def beside(step):
        return y * K + lax.rem(core + step, K), c

    barrier = pltpu.get_barrier_semaphore()
    greeted = [near(step, side) for step in range(plane) for side in range(K) if step or side]
    greeted += [(r, lax.rem(z + step, Z) * X + x) for step in range(1, Z)]
    for dev in greeted:
        pl.semaphore_signal(barrier, inc=1, device_id=dev, device_id_type=MESH)

    def part(ref, row, lane):
        return ref.at[pl.ds(pl.multiple_of((row * X + lane) * chunk, chunk), chunk), :]

    def mine(n):
        return part(ld_ref.at[n], r, x)

    def owner(n):
        i, j = LOWER[n]
        return i % R, j % C

    def scatter(n):
        for step in range(plane):
            for side in range(K):
                if step or side:
                    q, tc = near(step, side)
                    lane = lax.rem(tc, X)
                    yield pltpu.make_async_remote_copy(
                        src_ref=part(own_ref.at[n], q, lane), dst_ref=part(ld_ref.at[n], q, lane),
                        send_sem=scat_send.at[n, step * K + side], recv_sem=ld_sem.at[n],
                        device_id=(q, tc), device_id_type=MESH,
                    )

    for n in range(tiles):
        ri, cj = owner(n)

        @pl.when((r == ri) & (c == cj))
        def _():
            move_tile(own_ref.at[n], x_ref, LOWER[n][0] // R, LOWER[n][1] // C, B, T)
            mine(n)[...] = part(own_ref.at[n], r, x)[...]

    pl.semaphore_wait(barrier, len(greeted))
    for n in range(tiles):
        ri, cj = owner(n)

        @pl.when((r == ri) & (c == cj))
        def _():
            for copy in scatter(n):
                copy.start()

    def lead_out(n):
        zs = owner(n)[1] // X

        def line(m, to):
            return remote(mine(n), ld_send.at[n, m], ld_sem.at[n], (r, to * X + x))

        if n == 0:
            for to in range(Z):
                if to != zs:
                    yield z == zs, line(to, to)
        else:
            yield (z >= zs) & (z + 1 < Z), line(0, lax.rem(z + 1, Z))
            yield (z <= zs) & (z > 0), line(1, lax.rem(z + Z - 1, Z))
        for step in range(1, plane):
            yield r >= 0, remote(mine(n), ld_send.at[n, Z + step], ldp_sem.at[n, step], near(step))
        for side in range(1, K):
            yield r >= 0, remote(mine(n), ld_send.at[n, Z + plane + side], ldc_sem.at[n, side, 0], beside(side))

    def behind(n, step, side=0):
        ty, tx = lax.rem(y + Y - step // X, Y), lax.rem(x + X - step % X, X)
        return part(ld_ref.at[n], ty * K + lax.rem(core + K - side, K), tx)

    def lead_on(n, step):
        for side in range(1, K):
            m = Z + plane + K + (step - 1) * K + side
            yield remote(behind(n, step), ld_send.at[n, m], ldc_sem.at[n, side, step], beside(side))

    def lead_first(n):
        ri, cj = owner(n)
        pl.when((r != ri) | (c != cj))(lambda: arrived(mine(n), ld_sem.at[n]))
        for go, copy in lead_out(n):
            pl.when(go)(copy.start)

    def lead_second(n):
        for step in range(1, plane):
            arrived(behind(n, step), ldp_sem.at[n, step])
            for copy in lead_on(n, step):
                copy.start()

    def lead_third(n):
        for side in range(1, K):
            for step in range(plane):
                arrived(behind(n, step, side), ldc_sem.at[n, side, step])
        w_ref[n] = ld_ref[n]

    def lead_end(n):
        ri, cj = owner(n)

        @pl.when((r == ri) & (c == cj))
        def _():
            for copy in scatter(n):
                copy.wait_send()

        for go, copy in lead_out(n):
            pl.when(go)(copy.wait_send)
        for step in range(1, plane):
            for copy in lead_on(n, step):
                copy.wait_send()

    def item(m):
        tile, piece = lax.div(m, PIECES), lax.rem(m, PIECES)
        k, a = lax.div(tile, A), A - 1 - lax.rem(tile, A)
        source = lax.rem(k, C)
        zs, xs = lax.div(source, X), lax.rem(source, X)
        lane = lax.rem(k + a, X)
        return k, a, piece, source, zs, xs, lane

    def need(m):
        return item(m)[1] * R + r >= STEPS

    def piece_of(m):
        k, a, piece = item(m)[:3]
        rows = T // PIECES
        return rs_ref.at[k, a, pl.ds(pl.multiple_of(piece * rows, rows), rows), :]

    def spread(m):
        _, _, _, source, zs, xs, lane = item(m)
        on = (x == lane) & need(m)
        slot = piece_of(m)

        def copy(n, dev):
            return remote(slot, rs_send.at[m, n], rs_sem.at[m], dev)

        yield (c == source) & (xs != lane) & need(m), copy(0, (r, lax.rem(zs * X + lane, C)))
        yield on & (z >= zs) & (z + 1 < Z), copy(1, (r, lax.rem(c + X, C)))
        yield on & (z <= zs) & (z > 0), copy(2, (r, lax.rem(c + C - X, C)))
        for step in range(1, X):
            other = lax.rem(lane + step, X)
            yield on & jnp.logical_not((z == zs) & (other == xs)), copy(2 + step, (r, z * X + other))

    def forward(m):
        _, _, _, source, _, _, lane = item(m)

        @pl.when(((x == lane) | (c == source)) & need(m))
        def _():
            pl.when(c != source)(lambda: arrived(piece_of(m), rs_sem.at[m]))
            for go, out in spread(m):
                pl.when(go)(out.start)

    def col_at(e):
        k, b = lax.div(e, B), lax.rem(e, B)
        source = lax.rem(k, R)
        return cs_ref.at[k, b], source, lax.div(source, K), lax.rem(source, K)

    def col_out(e):
        slot, source, _, _ = col_at(e)
        for step in range(1, Y):
            yield r == source, remote(slot, cs_send.at[e, step - 1], cs_sem.at[e], across(step))

    def col_on(e):
        slot, _, _, kc = col_at(e)
        for step in range(1, K):
            yield core == kc, remote(slot, cs_send.at[e, Y + step - 2], cs_sem.at[e], beside(step))

    def col_first(e):
        for go, copy in col_out(e):
            pl.when(go)(copy.start)

    def col_second(e):
        slot, source, _, kc = col_at(e)

        @pl.when(core == kc)
        def _():
            pl.when(r != source)(lambda: arrived(slot, cs_sem.at[e]))
            for _, copy in col_on(e):
                copy.start()

    cols = STEPS * B
    rounds = A * PIECES

    def rows_work(u):
        for k in range(STEPS):
            source = k % C
            zs, xs = source // X, source % X
            v = u - RS_AT - k * GAP // STEPS - HOP * jnp.abs(z - zs)
            direct = lax.rem(v, GAP) == 0
            v = jnp.where(direct, v, v - HOP)
            h = lax.div(v, GAP)
            turned = lax.rem(k + A - 1 - lax.div(h, PIECES), X) != xs
            turn = jnp.logical_not(direct) & (lax.rem(v, GAP) == 0) & turned

            @pl.when((v >= 0) & (h < rounds) & (c != source) & (turn | (direct & jnp.logical_not(turned))))
            def _(k=k, h=h):
                forward(k * rounds + h)

    def lead_work(u):
        for n in range(1, tiles):
            pl.when((z == Z - 1) & (u == n - 1))(functools.partial(lead_first, n))
            pl.when(u == n + jnp.where(z == Z - 1, LATE, 0))(functools.partial(lead_second, n))

    def slot_work(u, k):
        if k == 0:
            lead_work(u)
        rows_work(u)
        e, f = u - CS_AT, u - CS_AT - CS_LAG
        pl.when((e >= 0) & (e < cols * CS_GAP) & (lax.rem(e, CS_GAP) == 0))(lambda: col_first(lax.div(e, CS_GAP)))
        pl.when((f >= 0) & (f < cols * CS_GAP) & (lax.rem(f, CS_GAP) == 0))(lambda: col_second(lax.div(f, CS_GAP)))

    lead_first(0)
    for k in range(STEPS):

        def own_rows(a, carry, k=k):
            pl.when(a * R + r >= STEPS)(lambda: move_tile(rs_ref.at[k, a], x_ref, a, k // C, B, T))
            return carry

        @pl.when(c == k % C)
        def _():
            lax.fori_loop(0, A, own_rows, 0)

        for b in range(B):
            pl.when(r == k % R)(lambda: move_tile(cs_ref.at[k, b], x_ref, k // R, b, B, T))
    for n in range(1, tiles):
        pl.when(z < Z - 1)(functools.partial(lead_first, n))
    for k in range(STEPS):

        @pl.when(c == k % C)
        def _(k=k):
            lax.fori_loop(0, rounds, lambda h, s: (forward(k * rounds + h), s)[1], 0)

    lead_second(0)
    lead_third(0)
    for k in range(STEPS):
        invert_factor(w_ref.at[SLOT[k, k]], lambda p, k=k: slot_work(k * blocks + p, k))
        inv = w_ref[SLOT[k, k]]
        if k == 0:
            for n in range(1, tiles):
                lead_third(n)
            for i in range(STEPS):

                @pl.when(r == i % R)
                def _():
                    for j in range(STEPS):
                        rs_ref[j, i // R] = ld_ref[SLOT[i, j]] if j <= i else jnp.zeros((T, T), F32)

        for i in range(k + 1, STEPS):
            w_ref[SLOT[i, k]] = dot_nt(w_ref[SLOT[i, k]], inv)
        for j in range(k + 1, STEPS):
            for i in range(j, STEPS):
                w_ref[SLOT[i, j]] = w_ref[SLOT[i, j]] - dot_nt(w_ref[SLOT[i, k]], w_ref[SLOT[j, k]])
    for k in range(STEPS):
        m_ref[SLOT[k, k]] = w_ref[SLOT[k, k]]
        for i in range(k + 1, STEPS):
            total = dot3(halves(w_ref[SLOT[i, k]]), halves(m_ref[SLOT[k, k]]), NN)
            for j in range(k + 1, i):
                total = total + dot3(halves(w_ref[SLOT[i, j]]), halves(m_ref[SLOT[j, k]]), NN)
            m_ref[SLOT[i, k]] = -dot3(halves(w_ref[SLOT[i, i]]), halves(total), NN)

    last = RS_AT + GAP * (rounds + 1) + HOP * Z
    last = max(last, CS_AT + CS_LAG + cols * CS_GAP)
    lax.fori_loop(STEPS * blocks, max(last, STEPS * blocks), lambda u, s: (slot_work(u, STEPS), s)[1], 0)

    def piece_out(m):
        k, a, piece = item(m)[:3]
        rows = T // PIECES
        dst = rs_out.at[k, a, pl.ds(pl.multiple_of(piece * rows, rows), rows), :]
        return pltpu.make_async_copy(piece_of(m), dst, out_sem.at[m])

    def col_copy(e):
        k, b = lax.div(e, B), lax.rem(e, B)
        return pltpu.make_async_copy(cs_ref.at[k, b], cs_out.at[k, b], col_sem.at[e])

    m_copy = pltpu.make_async_copy(m_ref, m_out, m_sem)
    m_copy.start()

    def item_here(m, carry):
        _, _, _, source, _, _, lane = item(m)
        pl.when((x != lane) & (c != source) & need(m))(lambda: arrived(piece_of(m), rs_sem.at[m]))
        piece_out(m).start()
        return carry

    def col_here(e, carry):
        slot, _, _, kc = col_at(e)
        pl.when(core != kc)(lambda: arrived(slot, cs_sem.at[e]))
        col_copy(e).start()
        return carry

    def item_end(m, carry):
        for go, out in spread(m):
            pl.when(go)(out.wait_send)
        piece_out(m).wait()
        return carry

    def col_end(e, carry):
        for copies in (col_out(e), col_on(e)):
            for go, copy in copies:
                pl.when(go)(copy.wait_send)
        col_copy(e).wait()
        return carry

    lax.fori_loop(0, cols, col_here, 0)
    lax.fori_loop(0, items, lambda m, s: item_here(lax.rem(m, STEPS) * rounds + lax.div(m, STEPS), s), 0)
    lax.fori_loop(0, items, item_end, 0)
    lax.fori_loop(0, cols, col_end, 0)
    m_copy.wait()
    for n in range(tiles):
        lead_end(n)


def lead(tiles, R, C, A, B, T):
    X, Z = split_col(C)
    K = 2 if R % 2 == 0 else 1
    Y = R // K
    plane = X * Y
    n = len(LOWER)
    items = STEPS * A * PIECES
    vmem = pl.BlockSpec(memory_space=pltpu.VMEM)
    hbm = pl.BlockSpec(memory_space=pl.ANY)
    dma = pltpu.SemaphoreType.DMA
    return pl.pallas_call(
        functools.partial(lead_kernel, R, C, A, B, T),
        name="lead",
        out_shape=(
            jax.ShapeDtypeStruct((n, T, T), F32),
            jax.ShapeDtypeStruct((STEPS, A, T, T), F32),
            jax.ShapeDtypeStruct((STEPS, B, T, T), F32),
        ),
        in_specs=[vmem],
        out_specs=(hbm, hbm, hbm),
        scratch_shapes=[
            pltpu.VMEM((n, T, T), F32),
            pltpu.VMEM((STEPS, A, T, T), F32),
            pltpu.VMEM((STEPS, B, T, T), F32),
            pltpu.VMEM((n, T, T), F32),
            pltpu.VMEM((n, T, T), F32),
            pltpu.VMEM((n, T, T), F32),
            dma(()), dma((items,)), dma((STEPS * B,)),
            dma((n, plane * K)), dma((n, Z + plane + K + plane * K)), dma((n,)), dma((n, plane)), dma((n, K, plane)),
            dma((items,)), dma((items, X + 2)), dma((STEPS * B,)), dma((STEPS * B, Y + K)),
        ],
        compiler_params=pltpu.CompilerParams(has_side_effects=True, collective_id=0, vmem_limit_bytes=56 * 2**20),
    )(tiles)


def halves(value):
    high = value.astype(BF16)
    return high, (value - high.astype(F32)).astype(BF16)


def dot3(p, q, dims):
    d = functools.partial(lax.dot_general, dimension_numbers=(dims, ((), ())), preferred_element_type=F32)
    return d(p[0], q[0]) + (d(p[0], q[1]) + d(p[1], q[0]))


NT = ((1,), (1,))
NN = ((1,), (0,))


def finish_kernel(R, C, A, B, T, x_ref, m_ref, rs_ref, cs_ref, t_ref, p_ref, mh_ref, ml_ref, qh_ref, ql_ref):
    H = T // LANES
    r, c = lax.axis_index("row"), lax.axis_index("col")
    a = pl.program_id(0)

    @pl.when(a == 0)
    def _():
        for n in range(len(LOWER)):
            mh_ref[n], ml_ref[n] = halves(m_ref[n])
        for b in range(B):
            terms = [halves(cs_ref[j, b]) for j in range(STEPS)]
            for k in range(STEPS):
                total = None
                for j in range(k + 1):
                    n = SLOT[k, j]
                    term = dot3((mh_ref[n], ml_ref[n]), terms[j], NN)
                    total = term if total is None else total + term
                qh_ref[k, b], ql_ref[k, b] = halves(total)

    tile_row = a * R + r
    terms = [halves(rs_ref[j, 0]) for j in range(STEPS)]
    panel = []
    for k in range(STEPS):
        total = None
        for j in range(k + 1):
            n = SLOT[k, j]
            term = dot3(terms[j], (mh_ref[n], ml_ref[n]), NT)
            total = term if total is None else total + term
        p_ref[0, k] = jnp.where(tile_row >= k, total, F32(0.0))
        panel.append(halves(total))
    for b in range(B):
        total = load_tile(x_ref, 0, b, B, T)
        for k in range(STEPS):
            total = total - dot3(panel[k], (qh_ref[k, b], ql_ref[k, b]), NN)
        keep = (tile_row >= STEPS) & (b * C + c >= STEPS)
        total = jnp.where(keep, total, F32(0.0))
        for h in range(H):
            t_ref[pl.ds(b * H + h, T, stride=B * H), :] = total[:, h * LANES : (h + 1) * LANES]


def finish(tiles, m, rs, cs, R, C, A, B, T):
    n = len(LOWER)
    rows = tiles.shape[0] // A
    flat = pl.BlockSpec((rows, LANES), lambda a: (a, 0))
    return pl.pallas_call(
        functools.partial(finish_kernel, R, C, A, B, T),
        name="finish",
        grid=(A,),
        out_shape=(jax.ShapeDtypeStruct(tiles.shape, F32), jax.ShapeDtypeStruct((A, STEPS, T, T), F32)),
        in_specs=[
            flat,
            pl.BlockSpec((n, T, T), lambda a: (0, 0, 0)),
            pl.BlockSpec((STEPS, 1, T, T), lambda a: (0, a, 0, 0)),
            pl.BlockSpec((STEPS, B, T, T), lambda a: (0, 0, 0, 0)),
        ],
        out_specs=(flat, pl.BlockSpec((1, STEPS, T, T), lambda a: (a, 0, 0, 0))),
        scratch_shapes=[
            pltpu.VMEM((n, T, T), BF16),
            pltpu.VMEM((n, T, T), BF16),
            pltpu.VMEM((STEPS, B, T, T), BF16),
            pltpu.VMEM((STEPS, B, T, T), BF16),
        ],
        compiler_params=pltpu.CompilerParams(vmem_limit_bytes=56 * 2**20),
    )(tiles, m, rs, cs)


def shards(kernel):
    A, _, T, B, _, _ = kernel.shape
    R, C = lax.axis_size("row"), lax.axis_size("col")
    tiles = kernel.reshape(-1, LANES)
    m, rs, cs = lead(tiles, R, C, A, B, T)
    trailing, panels = finish(tiles, m, rs, cs, R, C, A, B, T)
    return trailing.reshape(kernel.shape), panels.transpose(0, 2, 1, 3).reshape(A, 1, T, STEPS, T)


def solution(mesh):
    in_specs = (P(None, "row", None, None, "col", None),)
    out_specs = (P(None, "row", None, None, "col", None), P(None, "row", None, None, None))
    return jax.shard_map(shards, mesh=mesh, in_specs=in_specs, out_specs=out_specs, check_vma=False)
```

```python
import functools

import jax
import jax.numpy as jnp
from jax import lax
from jax.experimental import pallas as pl
from jax.experimental.pallas import tpu as pltpu
from jax.sharding import PartitionSpec as P

STEPS = 3
PANEL = 16
LANES = 128
GROUPS = 4
EVERY = 2
LATE = 2
RS_AT = -5
GAP = 2
HOP = 5
CS_AT = 4
CS_GAP = 2
CS_LAG = 4
PIECES = 2
MESH = pl.DeviceIdType.MESH
F32 = jnp.float32
BF16 = jnp.bfloat16
LOWER = [(i, j) for j in range(STEPS) for i in range(j, STEPS)]
SLOT = {ij: n for n, ij in enumerate(LOWER)}


def split_col(cols):
    width = 1
    while width * width * 4 <= cols:
        width *= 2
    return width, cols // width


def dot_nt(p, q):
    return lax.dot_general(p, q, (((1,), (1,)), ((), ())), precision=lax.Precision.HIGHEST, preferred_element_type=F32)


def invert_factor(w_ref, between):
    T = w_ref.shape[0]
    b, half = PANEL, PANEL // 2
    lane = lax.broadcasted_iota(jnp.int32, (b, T), 1)
    sub = lax.broadcasted_iota(jnp.int32, (b, T), 0)
    row = lax.broadcasted_iota(jnp.int32, (T, T), 0)
    col = lax.broadcasted_iota(jnp.int32, (T, T), 1)
    wide = T // LANES
    narrow = lax.broadcasted_iota(jnp.int32, (half, LANES), 0)
    zero = F32(0.0)

    def spread(value):
        return jnp.concatenate([value] * wide, axis=1)

    def body(p, first):
        base = pl.multiple_of(p * b, b)
        R = w_ref[pl.ds(base, b), :]
        cols = []
        for j in range(b):
            picked = jnp.sum(jnp.where(lane == base + j, R, zero), axis=1, keepdims=True)
            cols.append([jnp.broadcast_to(picked[h * half : (h + 1) * half], (half, LANES)) for h in range(2)])
        V = jnp.where((lane >= base) & (lane < base + b), jnp.where(lane == base + sub, F32(1.0), zero), R)
        V = [V[:half], V[half:]]
        diag = [jnp.ones((half, LANES), F32) for _ in range(2)]
        for j in range(b):
            own, at = divmod(j, half)
            d = jnp.broadcast_to(cols[j][own][at : at + 1, :], (half, LANES))
            diag[own] = jnp.where(narrow == at, d, diag[own])
            if j == b - 1:
                break
            inverse = F32(1.0) / d
            pivot = V[own][at : at + 1, :]
            for h in range(own, 2):
                w = cols[j][h] * inverse
                if h == own:
                    w = jnp.where(narrow > at, w, zero)
                V[h] = V[h] - spread(w) * pivot
                for i in range(j + 1, b):
                    cols[i][h] = cols[i][h] - w * cols[i][own][at : at + 1, :] if h > own else cols[i][h]
            w = jnp.where(narrow > at, cols[j][own] * inverse, zero)
            for i in range(j + 1, b):
                cols[i][own] = cols[i][own] - w * cols[i][own][at : at + 1, :]
        V = jnp.concatenate([v * spread(lax.rsqrt(d)) for v, d in zip(V, diag)], axis=0)
        coef = jnp.where(lane >= base + b, V, zero)
        update = lax.dot_general(
            coef[:, first:], V, (((0,), (0,)), ((), ())), precision=lax.Precision.HIGHEST, preferred_element_type=F32
        )
        drop = (row[first:] >= base + b) & (col[first:] >= base) & (col[first:] < base + b)
        w_ref[first:, :] = jnp.where(drop, zero, w_ref[first:, :]) - update
        w_ref[pl.ds(base, b), :] = V

    step = T // GROUPS

    for g in range(GROUPS):

        def block(q, carry, first=g * step):
            between(q)
            for p in range(EVERY):
                body(q * EVERY + p, first)
            return carry

        lax.fori_loop(g * step // b // EVERY, (g + 1) * step // b // EVERY, block, 0)
    w_ref[...] = jnp.where(row >= col, w_ref[...], zero)


def read_tile(x_ref, a, b, B, T):
    halves_ = T // LANES
    stride = B * halves_
    start = a * (T * stride) + b * halves_
    return [x_ref[pl.ds(start + h, T, stride=stride), :] for h in range(halves_)]


def load_tile(x_ref, a, b, B, T):
    return jnp.concatenate(read_tile(x_ref, a, b, B, T), axis=1)


def move_tile(dst, x_ref, a, b, B, T):
    for h, value in enumerate(read_tile(x_ref, a, b, B, T)):
        dst[:, h * LANES : (h + 1) * LANES] = value


def lead_kernel(
    R, C, A, B, T, x_ref, m_out, rs_out, cs_out, m_ref, rs_ref, cs_ref, own_ref, ld_ref, w_ref, m_sem, out_sem, col_sem,
    scat_send, ld_send, ld_sem, ldp_sem, ldc_sem, rs_sem, rs_send, cs_sem, cs_send,
):
    X, Z = split_col(C)
    K = 2 if R % 2 == 0 else 1
    Y = R // K
    r, c = lax.axis_index("row"), lax.axis_index("col")
    z, x = lax.div(c, X), lax.rem(c, X)
    y, core = lax.div(r, K), lax.rem(r, K)
    plane = Y * X
    chunk = T // (R * X)
    items = A * STEPS * PIECES
    tiles = len(LOWER)
    blocks = T // PANEL // EVERY

    def remote(src, send_sem, recv_sem, dev):
        return pltpu.make_async_remote_copy(
            src_ref=src, dst_ref=src, send_sem=send_sem, recv_sem=recv_sem, device_id=dev, device_id_type=MESH
        )

    def arrived(dst, recv_sem):
        remote(dst, scat_send.at[0, 0], recv_sem, (lax.rem(r + 1, R), c)).wait_recv()

    def near(step, side=0):
        ty, tx = lax.rem(y + step // X, Y), lax.rem(x + step % X, X)
        return ty * K + lax.rem(core + side, K), z * X + tx

    def across(step):
        return lax.rem(y + step, Y) * K + core, c

    def beside(step):
        return y * K + lax.rem(core + step, K), c

    barrier = pltpu.get_barrier_semaphore()
    greeted = [near(step, side) for step in range(plane) for side in range(K) if step or side]
    greeted += [(r, lax.rem(z + step, Z) * X + x) for step in range(1, Z)]
    for dev in greeted:
        pl.semaphore_signal(barrier, inc=1, device_id=dev, device_id_type=MESH)

    def part(ref, row, lane):
        return ref.at[pl.ds(pl.multiple_of((row * X + lane) * chunk, chunk), chunk), :]

    def mine(n):
        return part(ld_ref.at[n], r, x)

    def owner(n):
        i, j = LOWER[n]
        return i % R, j % C

    def scatter(n):
        for step in range(plane):
            for side in range(K):
                if step or side:
                    q, tc = near(step, side)
                    lane = lax.rem(tc, X)
                    yield pltpu.make_async_remote_copy(
                        src_ref=part(own_ref.at[n], q, lane), dst_ref=part(ld_ref.at[n], q, lane),
                        send_sem=scat_send.at[n, step * K + side], recv_sem=ld_sem.at[n],
                        device_id=(q, tc), device_id_type=MESH,
                    )

    for n in range(tiles):
        ri, cj = owner(n)

        @pl.when((r == ri) & (c == cj))
        def _():
            move_tile(own_ref.at[n], x_ref, LOWER[n][0] // R, LOWER[n][1] // C, B, T)
            mine(n)[...] = part(own_ref.at[n], r, x)[...]

    pl.semaphore_wait(barrier, len(greeted))
    for n in range(tiles):
        ri, cj = owner(n)

        @pl.when((r == ri) & (c == cj))
        def _():
            for copy in scatter(n):
                copy.start()

    def lead_out(n):
        zs = owner(n)[1] // X

        def line(m, to):
            return remote(mine(n), ld_send.at[n, m], ld_sem.at[n], (r, to * X + x))

        if n == 0:
            for to in range(Z):
                if to != zs:
                    yield z == zs, line(to, to)
        else:
            yield (z >= zs) & (z + 1 < Z), line(0, lax.rem(z + 1, Z))
            yield (z <= zs) & (z > 0), line(1, lax.rem(z + Z - 1, Z))
        for step in range(1, plane):
            yield r >= 0, remote(mine(n), ld_send.at[n, Z + step], ldp_sem.at[n, step], near(step))
        for side in range(1, K):
            yield r >= 0, remote(mine(n), ld_send.at[n, Z + plane + side], ldc_sem.at[n, side, 0], beside(side))

    def behind(n, step, side=0):
        ty, tx = lax.rem(y + Y - step // X, Y), lax.rem(x + X - step % X, X)
        return part(ld_ref.at[n], ty * K + lax.rem(core + K - side, K), tx)

    def lead_on(n, step):
        for side in range(1, K):
            m = Z + plane + K + (step - 1) * K + side
            yield remote(behind(n, step), ld_send.at[n, m], ldc_sem.at[n, side, step], beside(side))

    def lead_first(n):
        ri, cj = owner(n)
        pl.when((r != ri) | (c != cj))(lambda: arrived(mine(n), ld_sem.at[n]))
        for go, copy in lead_out(n):
            pl.when(go)(copy.start)

    def lead_second(n):
        for step in range(1, plane):
            arrived(behind(n, step), ldp_sem.at[n, step])
            for copy in lead_on(n, step):
                copy.start()

    def lead_third(n):
        for side in range(1, K):
            for step in range(plane):
                arrived(behind(n, step, side), ldc_sem.at[n, side, step])
        w_ref[n] = ld_ref[n]

    def lead_end(n):
        ri, cj = owner(n)

        @pl.when((r == ri) & (c == cj))
        def _():
            for copy in scatter(n):
                copy.wait_send()

        for go, copy in lead_out(n):
            pl.when(go)(copy.wait_send)
        for step in range(1, plane):
            for copy in lead_on(n, step):
                copy.wait_send()

    def item(m):
        tile, piece = lax.div(m, PIECES), lax.rem(m, PIECES)
        k, a = lax.div(tile, A), A - 1 - lax.rem(tile, A)
        source = lax.rem(k, C)
        zs, xs = lax.div(source, X), lax.rem(source, X)
        lane = lax.rem(k + a + 1, X)
        return k, a, piece, source, zs, xs, lane

    def need(m):
        return item(m)[1] * R + r >= STEPS

    def piece_of(m):
        k, a, piece = item(m)[:3]
        rows = T // PIECES
        return rs_ref.at[k, a, pl.ds(pl.multiple_of(piece * rows, rows), rows), :]

    def spread(m):
        _, _, _, source, zs, xs, lane = item(m)
        on = (x == lane) & need(m)
        slot = piece_of(m)

        def copy(n, dev):
            return remote(slot, rs_send.at[m, n], rs_sem.at[m], dev)

        yield (c == source) & (xs != lane) & need(m), copy(0, (r, lax.rem(zs * X + lane, C)))
        yield on & (z >= zs) & (z + 1 < Z), copy(1, (r, lax.rem(c + X, C)))
        yield on & (z <= zs) & (z > 0), copy(2, (r, lax.rem(c + C - X, C)))
        for step in range(1, X):
            other = lax.rem(lane + step, X)
            yield on & jnp.logical_not((z == zs) & (other == xs)), copy(2 + step, (r, z * X + other))

    def forward(m):
        _, _, _, source, _, _, lane = item(m)

        @pl.when(((x == lane) | (c == source)) & need(m))
        def _():
            pl.when(c != source)(lambda: arrived(piece_of(m), rs_sem.at[m]))
            for go, out in spread(m):
                pl.when(go)(out.start)

    def col_at(e):
        k, b = lax.div(e, B), lax.rem(e, B)
        source = lax.rem(k, R)
        return cs_ref.at[k, b], source, lax.div(source, K), lax.rem(source, K)

    def col_out(e):
        slot, source, _, _ = col_at(e)
        for step in range(1, Y):
            yield r == source, remote(slot, cs_send.at[e, step - 1], cs_sem.at[e], across(step))

    def col_on(e):
        slot, _, _, kc = col_at(e)
        for step in range(1, K):
            yield core == kc, remote(slot, cs_send.at[e, Y + step - 2], cs_sem.at[e], beside(step))

    def col_first(e):
        for go, copy in col_out(e):
            pl.when(go)(copy.start)

    def col_second(e):
        slot, source, _, kc = col_at(e)

        @pl.when(core == kc)
        def _():
            pl.when(r != source)(lambda: arrived(slot, cs_sem.at[e]))
            for _, copy in col_on(e):
                copy.start()

    cols = STEPS * B
    rounds = A * PIECES

    def rows_work(u):
        for k in range(STEPS):
            source = k % C
            zs, xs = source // X, source % X
            v = u - RS_AT - k * GAP // STEPS - HOP * jnp.abs(z - zs)
            direct = lax.rem(v, GAP) == 0
            v = jnp.where(direct, v, v - HOP)
            h = lax.div(v, GAP)
            turned = lax.rem(k + A - lax.div(h, PIECES), X) != xs
            turn = jnp.logical_not(direct) & (lax.rem(v, GAP) == 0) & turned

            @pl.when((v >= 0) & (h < rounds) & (c != source) & (turn | (direct & jnp.logical_not(turned))))
            def _(k=k, h=h):
                forward(k * rounds + h)

    def lead_work(u):
        for n in range(1, tiles):
            pl.when((z == Z - 1) & (u == n - 1))(functools.partial(lead_first, n))
            pl.when(u == n + jnp.where(z == Z - 1, LATE, 0))(functools.partial(lead_second, n))

    def slot_work(u, k):
        if k == 0:
            lead_work(u)
        rows_work(u)
        e, f = u - CS_AT, u - CS_AT - CS_LAG
        pl.when((e >= 0) & (e < cols * CS_GAP) & (lax.rem(e, CS_GAP) == 0))(lambda: col_first(lax.div(e, CS_GAP)))
        pl.when((f >= 0) & (f < cols * CS_GAP) & (lax.rem(f, CS_GAP) == 0))(lambda: col_second(lax.div(f, CS_GAP)))

    lead_first(0)
    for k in range(STEPS):

        def own_rows(a, carry, k=k):
            pl.when(a * R + r >= STEPS)(lambda: move_tile(rs_ref.at[k, a], x_ref, a, k // C, B, T))
            return carry

        @pl.when(c == k % C)
        def _():
            lax.fori_loop(0, A, own_rows, 0)

        for b in range(B):
            pl.when(r == k % R)(lambda: move_tile(cs_ref.at[k, b], x_ref, k // R, b, B, T))
    for n in range(1, tiles):
        pl.when(z < Z - 1)(functools.partial(lead_first, n))
    for k in range(STEPS):

        @pl.when(c == k % C)
        def _(k=k):
            lax.fori_loop(0, rounds, lambda h, s: (forward(k * rounds + h), s)[1], 0)

    lead_second(0)
    lead_third(0)
    for k in range(STEPS):
        invert_factor(w_ref.at[SLOT[k, k]], lambda p, k=k: slot_work(k * blocks + p, k))
        inv = w_ref[SLOT[k, k]]
        if k == 0:
            for n in range(1, tiles):
                lead_third(n)
            for i in range(STEPS):

                @pl.when(r == i % R)
                def _():
                    for j in range(STEPS):
                        rs_ref[j, i // R] = ld_ref[SLOT[i, j]] if j <= i else jnp.zeros((T, T), F32)

        for i in range(k + 1, STEPS):
            w_ref[SLOT[i, k]] = dot_nt(w_ref[SLOT[i, k]], inv)
        for j in range(k + 1, STEPS):
            for i in range(j, STEPS):
                w_ref[SLOT[i, j]] = w_ref[SLOT[i, j]] - dot_nt(w_ref[SLOT[i, k]], w_ref[SLOT[j, k]])
    for k in range(STEPS):
        m_ref[SLOT[k, k]] = w_ref[SLOT[k, k]]
        for i in range(k + 1, STEPS):
            total = dot3(halves(w_ref[SLOT[i, k]]), halves(m_ref[SLOT[k, k]]), NN)
            for j in range(k + 1, i):
                total = total + dot3(halves(w_ref[SLOT[i, j]]), halves(m_ref[SLOT[j, k]]), NN)
            m_ref[SLOT[i, k]] = -dot3(halves(w_ref[SLOT[i, i]]), halves(total), NN)

    last = RS_AT + GAP * (rounds + 1) + HOP * Z
    last = max(last, CS_AT + CS_LAG + cols * CS_GAP)
    lax.fori_loop(STEPS * blocks, max(last, STEPS * blocks), lambda u, s: (slot_work(u, STEPS), s)[1], 0)

    def piece_out(m):
        k, a, piece = item(m)[:3]
        rows = T // PIECES
        dst = rs_out.at[k, a, pl.ds(pl.multiple_of(piece * rows, rows), rows), :]
        return pltpu.make_async_copy(piece_of(m), dst, out_sem.at[m])

    def col_copy(e):
        k, b = lax.div(e, B), lax.rem(e, B)
        return pltpu.make_async_copy(cs_ref.at[k, b], cs_out.at[k, b], col_sem.at[e])

    m_copy = pltpu.make_async_copy(m_ref, m_out, m_sem)
    m_copy.start()

    def item_here(m, carry):
        _, _, _, source, _, _, lane = item(m)
        pl.when((x != lane) & (c != source) & need(m))(lambda: arrived(piece_of(m), rs_sem.at[m]))
        piece_out(m).start()
        return carry

    def col_here(e, carry):
        slot, _, _, kc = col_at(e)
        pl.when(core != kc)(lambda: arrived(slot, cs_sem.at[e]))
        col_copy(e).start()
        return carry

    def item_end(m, carry):
        for go, out in spread(m):
            pl.when(go)(out.wait_send)
        piece_out(m).wait()
        return carry

    def col_end(e, carry):
        for copies in (col_out(e), col_on(e)):
            for go, copy in copies:
                pl.when(go)(copy.wait_send)
        col_copy(e).wait()
        return carry

    lax.fori_loop(0, cols, col_here, 0)
    lax.fori_loop(0, items, lambda m, s: item_here(lax.rem(m, STEPS) * rounds + lax.div(m, STEPS), s), 0)
    lax.fori_loop(0, items, item_end, 0)
    lax.fori_loop(0, cols, col_end, 0)
    m_copy.wait()
    for n in range(tiles):
        lead_end(n)


def lead(tiles, R, C, A, B, T):
    X, Z = split_col(C)
    K = 2 if R % 2 == 0 else 1
    Y = R // K
    plane = X * Y
    n = len(LOWER)
    items = STEPS * A * PIECES
    vmem = pl.BlockSpec(memory_space=pltpu.VMEM)
    hbm = pl.BlockSpec(memory_space=pl.ANY)
    dma = pltpu.SemaphoreType.DMA
    return pl.pallas_call(
        functools.partial(lead_kernel, R, C, A, B, T),
        name="lead",
        out_shape=(
            jax.ShapeDtypeStruct((n, T, T), F32),
            jax.ShapeDtypeStruct((STEPS, A, T, T), F32),
            jax.ShapeDtypeStruct((STEPS, B, T, T), F32),
        ),
        in_specs=[vmem],
        out_specs=(hbm, hbm, hbm),
        scratch_shapes=[
            pltpu.VMEM((n, T, T), F32),
            pltpu.VMEM((STEPS, A, T, T), F32),
            pltpu.VMEM((STEPS, B, T, T), F32),
            pltpu.VMEM((n, T, T), F32),
            pltpu.VMEM((n, T, T), F32),
            pltpu.VMEM((n, T, T), F32),
            dma(()), dma((items,)), dma((STEPS * B,)),
            dma((n, plane * K)), dma((n, Z + plane + K + plane * K)), dma((n,)), dma((n, plane)), dma((n, K, plane)),
            dma((items,)), dma((items, X + 2)), dma((STEPS * B,)), dma((STEPS * B, Y + K)),
        ],
        compiler_params=pltpu.CompilerParams(has_side_effects=True, collective_id=0, vmem_limit_bytes=56 * 2**20),
    )(tiles)


def halves(value):
    high = value.astype(BF16)
    return high, (value - high.astype(F32)).astype(BF16)


def dot3(p, q, dims):
    d = functools.partial(lax.dot_general, dimension_numbers=(dims, ((), ())), preferred_element_type=F32)
    return d(p[0], q[0]) + (d(p[0], q[1]) + d(p[1], q[0]))


NT = ((1,), (1,))
NN = ((1,), (0,))


def finish_kernel(R, C, A, B, T, x_ref, m_ref, rs_ref, cs_ref, t_ref, p_ref, mh_ref, ml_ref, qh_ref, ql_ref):
    H = T // LANES
    r, c = lax.axis_index("row"), lax.axis_index("col")
    a = pl.program_id(0)

    @pl.when(a == 0)
    def _():
        for n in range(len(LOWER)):
            mh_ref[n], ml_ref[n] = halves(m_ref[n])
        for b in range(B):
            terms = [halves(cs_ref[j, b]) for j in range(STEPS)]
            for k in range(STEPS):
                total = None
                for j in range(k + 1):
                    n = SLOT[k, j]
                    term = dot3((mh_ref[n], ml_ref[n]), terms[j], NN)
                    total = term if total is None else total + term
                qh_ref[k, b], ql_ref[k, b] = halves(total)

    tile_row = a * R + r
    terms = [halves(rs_ref[j, 0]) for j in range(STEPS)]
    panel = []
    for k in range(STEPS):
        total = None
        for j in range(k + 1):
            n = SLOT[k, j]
            term = dot3(terms[j], (mh_ref[n], ml_ref[n]), NT)
            total = term if total is None else total + term
        p_ref[0, k] = jnp.where(tile_row >= k, total, F32(0.0))
        panel.append(halves(total))
    for b in range(B):
        total = load_tile(x_ref, 0, b, B, T)
        for k in range(STEPS):
            total = total - dot3(panel[k], (qh_ref[k, b], ql_ref[k, b]), NN)
        keep = (tile_row >= STEPS) & (b * C + c >= STEPS)
        total = jnp.where(keep, total, F32(0.0))
        for h in range(H):
            t_ref[pl.ds(b * H + h, T, stride=B * H), :] = total[:, h * LANES : (h + 1) * LANES]


def finish(tiles, m, rs, cs, R, C, A, B, T):
    n = len(LOWER)
    rows = tiles.shape[0] // A
    flat = pl.BlockSpec((rows, LANES), lambda a: (a, 0))
    return pl.pallas_call(
        functools.partial(finish_kernel, R, C, A, B, T),
        name="finish",
        grid=(A,),
        out_shape=(jax.ShapeDtypeStruct(tiles.shape, F32), jax.ShapeDtypeStruct((A, STEPS, T, T), F32)),
        in_specs=[
            flat,
            pl.BlockSpec((n, T, T), lambda a: (0, 0, 0)),
            pl.BlockSpec((STEPS, 1, T, T), lambda a: (0, a, 0, 0)),
            pl.BlockSpec((STEPS, B, T, T), lambda a: (0, 0, 0, 0)),
        ],
        out_specs=(flat, pl.BlockSpec((1, STEPS, T, T), lambda a: (a, 0, 0, 0))),
        scratch_shapes=[
            pltpu.VMEM((n, T, T), BF16),
            pltpu.VMEM((n, T, T), BF16),
            pltpu.VMEM((STEPS, B, T, T), BF16),
            pltpu.VMEM((STEPS, B, T, T), BF16),
        ],
        compiler_params=pltpu.CompilerParams(vmem_limit_bytes=56 * 2**20),
    )(tiles, m, rs, cs)


def shards(kernel):
    A, _, T, B, _, _ = kernel.shape
    R, C = lax.axis_size("row"), lax.axis_size("col")
    tiles = kernel.reshape(-1, LANES)
    m, rs, cs = lead(tiles, R, C, A, B, T)
    trailing, panels = finish(tiles, m, rs, cs, R, C, A, B, T)
    return trailing.reshape(kernel.shape), panels.transpose(0, 2, 1, 3).reshape(A, 1, T, STEPS, T)


def solution(mesh):
    in_specs = (P(None, "row", None, None, "col", None),)
    out_specs = (P(None, "row", None, None, "col", None), P(None, "row", None, None, None))
    return jax.shard_map(shards, mesh=mesh, in_specs=in_specs, out_specs=out_specs, check_vma=False)
```
